256 devices in a mesh: dp: 8 (over y, z_hi), tm: 4 (over x), height: 8 (over z_lo, core).
Axes of the slice: x: 4, y: 4, z: 8 (z_hi: 2, z_lo: 4; z = z_hi * 4 + z_lo), core: 2. Of those that a mesh axis runs over, the one named last changes fastest.
Arguments:
- low_frames: bfloat16 [8, 16, 32, 32, 256], P('dp', 'tm', 'height'), may hold values from -6 to 6
- spatial_weight: bfloat16 [3, 3, 256, 256], replicated, may hold values from -0.125 to 0.125
- temporal_weight: bfloat16 [3, 256, 256], replicated, may hold values from -0.21875 to 0.21875
- cotangent: bfloat16 [8, 16, 64, 64, 256], P('dp', 'tm', 'height'), may hold values from -6 to 6
Outputs:
- section_out: bfloat16 [8, 16, 64, 64, 256], P('dp', 'tm', 'height')
- input_grad: bfloat16 [8, 16, 32, 32, 256], P('dp', 'tm', 'height')
- spatial_grad: float32 [3, 3, 256, 256], replicated
- temporal_grad: float32 [3, 256, 256], replicated
The draws below stay inside these ranges and needn't reach their ends.
All inputs are finite; a program needn't handle non-finite values.
Results may differ from the reference program's by a relative error of at most 0.0033.
Values may be sent and summed in bfloat16 or wider, within the bound.
A program may use at most 64 MiB of HBM per device.

```python
import jax
import jax.numpy as jnp
from jax import lax

C = 256
WL = 32
CLIPS = 8
FRAMES = 16
ROWS_IN = 32


def block_scale(key, dims, shards, low, high):
    factor_of, own = 1.0, jax.random.fold_in(key, 6)
    for axis_at, parts in shards:
        draws = jnp.exp(jax.random.uniform(jax.random.fold_in(own, axis_at), (parts,), jnp.float32, low / len(shards), high / len(shards)))
        factor_of = factor_of * jnp.repeat(draws, dims[axis_at] // parts).reshape([-1 if axis == axis_at else 1 for axis in range(len(dims))])
    return factor_of


def normal_values(stream_key, dims, deviation, most, shards=(), held_as=jnp.bfloat16):
    entries = jax.random.normal(stream_key, dims, jnp.float32) * deviation
    if len(shards) > 0:
        entries = block_scale(stream_key, dims, shards, -0.22, 0.18) * entries
    return jnp.clip(entries, min=-most, max=most).astype(held_as)


def setup_inputs(seed: int = 0) -> dict:
    keys = jax.random.split(jax.random.key(seed), 5)
    low_frames = normal_values(keys[0], (CLIPS, FRAMES, ROWS_IN, WL, C), 1.0, 6.0, ((0, 8), (1, 4), (2, 8)))
    spatial_weight = normal_values(keys[1], (3, 3, C, C), (9 * C) ** -0.5, 0.125)
    temporal_weight = normal_values(keys[2], (3, C, C), (3 * C) ** -0.5, 0.21875)
    cotangent = normal_values(keys[3], (CLIPS, FRAMES, 2 * ROWS_IN, 2 * WL, C), 1.0, 6.0, ((0, 8), (1, 4), (2, 8)))
    return dict(low_frames=low_frames, spatial_weight=spatial_weight, temporal_weight=temporal_weight, cotangent=cotangent)


def spatial_apply(padded, weights, rows, cols):
    chan = weights.shape[-1]
    total = jnp.zeros((padded.shape[0] * rows * cols, chan), jnp.float32)
    for i in range(3):
        for j in range(3):
            piece = padded[:, i:i + rows, j:j + cols, :].reshape(-1, chan)
            total = total + jnp.dot(piece, weights[i, j], preferred_element_type=jnp.float32)
    return total


def one_clip(args):
    low, spatial_weight, temporal_weight, grad_out = args
    frames, rows_low, cols_low, chan = low.shape
    rows = 2 * rows_low
    cols = 2 * cols_low
    upsampled = jnp.repeat(jnp.repeat(low, 2, axis=1), 2, axis=2)
    padded = jnp.pad(upsampled, ((0, 0), (1, 1), (1, 1), (0, 0)))
    pre = spatial_apply(padded, spatial_weight, rows, cols)
    act = jax.nn.silu(pre).astype(jnp.bfloat16).reshape(frames, rows, cols, chan)
    act_ext = jnp.concatenate([jnp.zeros((2, rows, cols, chan), jnp.bfloat16), act], 0)
    mixed = upsampled.reshape(-1, chan).astype(jnp.float32)
    for k in range(3):
        mixed = mixed + jnp.dot(act_ext[2 - k:2 - k + frames].reshape(-1, chan), temporal_weight[k], preferred_element_type=jnp.float32)
    section_out = mixed.astype(jnp.bfloat16).reshape(frames, rows, cols, chan)
    grad_ext = jnp.concatenate([grad_out, jnp.zeros((2, rows, cols, chan), jnp.bfloat16)], 0)
    grad_flat = grad_out.reshape(-1, chan)
    act_grad = jnp.zeros((frames * rows * cols, chan), jnp.float32)
    tgrads = []
    for k in range(3):
        act_grad = act_grad + jnp.dot(grad_ext[k:k + frames].reshape(-1, chan), temporal_weight[k].T, preferred_element_type=jnp.float32)
        tgrads.append(lax.dot_general(act_ext[2 - k:2 - k + frames].reshape(-1, chan), grad_flat, (((0,), (0,)), ((), ())), preferred_element_type=jnp.float32))
    sig = jax.nn.sigmoid(pre)
    pre_grad = (act_grad * (sig * (1.0 + pre * (1.0 - sig)))).astype(jnp.bfloat16)
    sgrads = []
    for i in range(3):
        for j in range(3):
            piece = padded[:, i:i + rows, j:j + cols, :].reshape(-1, chan)
            sgrads.append(lax.dot_general(piece, pre_grad, (((0,), (0,)), ((), ())), preferred_element_type=jnp.float32))
    grad_pad = jnp.pad(pre_grad.reshape(frames, rows, cols, chan), ((0, 0), (1, 1), (1, 1), (0, 0)))
    total = grad_out.reshape(-1, chan).astype(jnp.float32)
    for i in range(3):
        for j in range(3):
            piece = grad_pad[:, 2 - i:2 - i + rows, 2 - j:2 - j + cols, :].reshape(-1, chan)
            total = total + jnp.dot(piece, spatial_weight[i, j].T, preferred_element_type=jnp.float32)
    input_grad = total.reshape(frames, rows_low, 2, cols_low, 2, chan).sum(axis=(2, 4)).astype(jnp.bfloat16)
    return section_out, input_grad, jnp.stack(sgrads).reshape(3, 3, chan, chan), jnp.stack(tgrads)


def reference(low_frames, spatial_weight, temporal_weight, cotangent):
    clips = low_frames.shape[0]
    outs = []
    grads_in = []
    sgrad = jnp.zeros(spatial_weight.shape, jnp.float32)
    tgrad = jnp.zeros(temporal_weight.shape, jnp.float32)
    for clip in range(clips):
        section_out, input_grad, sg, tg = one_clip((low_frames[clip], spatial_weight, temporal_weight, cotangent[clip]))
        outs.append(section_out)
        grads_in.append(input_grad)
        sgrad = sgrad + sg
        tgrad = tgrad + tg
    return jnp.stack(outs), jnp.stack(grads_in), sgrad, tgrad
```

```python
import jax
import jax.numpy as jnp
from jax import lax
from jax.sharding import PartitionSpec as P
from jax.experimental import pallas as pl
from jax.experimental.pallas import tpu as pltpu

F32 = jnp.float32
BF16 = jnp.bfloat16
MESH = pl.DeviceIdType.MESH
N0, N1, N2, N3 = 192, 24, 6, 3


def place():
    dp, tm, h = lax.axis_index("dp"), lax.axis_index("tm"), lax.axis_index("height")
    return dict(x=tm, y=dp // 2, z=(dp % 2) * 4 + h // 2, c=h % 2)


def device(p):
    return (p["y"] * 2 + p["z"] // 4, p["x"], (p["z"] % 4) * 2 + p["c"])


SIZE = dict(x=4, y=4, z=8, c=2)


def peer(me, axis, d):
    return {**me, axis: (me[axis] + d) % SIZE[axis]}


def partners(me):
    return [peer(me, axis, d) for axis in ("c", "x", "y", "z") for d in range(1, SIZE[axis])]


AR_SCRATCH = [
    pltpu.VMEM((N0, 8, 256), F32),
    pltpu.VMEM((N0, 8, 256), F32),
    pltpu.VMEM((N0, 8, 256), BF16),
    pltpu.VMEM((2, 3, N1, 8, 256), BF16),
    pltpu.VMEM((2, N1, 8, 256), F32),
    pltpu.VMEM((2, 3, N2, 8, 256), F32),
    pltpu.VMEM((2, N2, 8, 256), F32),
    pltpu.VMEM((7, N3, 8, 128), F32),
    pltpu.VMEM((2 * N0, 8, 256), BF16),
    pltpu.SemaphoreType.DMA((40,)),
    pltpu.SemaphoreType.DMA((40,)),
]


def loop(count, body):
    def step(i, carry):
        body(i)
        return carry

    lax.fori_loop(0, count, step, 0)


def ar_kernel(x_ref, s_out, t_out, recv0, acc, snd1, recv1, acc1, recv2, acc2, recv3, full, ssem, rsem):
    me = place()
    barrier = pltpu.get_barrier_semaphore()
    others = partners(me)
    for p in others:
        pl.semaphore_signal(barrier, inc=1, device_id=device(p), device_id_type=MESH)
    pl.semaphore_wait(barrier, len(others))
    used = [0]

    def send(src, dst, to):
        k = used[0]
        used[0] += 1
        copy = pltpu.make_async_remote_copy(
            src_ref=src, dst_ref=dst, send_sem=ssem.at[k], recv_sem=rsem.at[k],
            device_id=device(to), device_id_type=MESH,
        )
        copy.start()
        return copy

    started = []

    def exchange(copies):
        started.extend(copies)
        for c in copies:
            c.wait_recv()

    c = me["c"]
    exchange([send(x_ref.at[pl.ds((1 - c) * N0, N0)], recv0, peer(me, "c", 1))])

    def add0(i):
        at = pl.ds(i * 12, 12)
        total = x_ref[pl.ds(c * N0 + i * 12, 12)] + recv0[at]
        acc[at] = total
        snd1[at] = total.astype(BF16)

    loop(16, add0)
    order = (("x", "y"), ("y", "x"))
    copies = []
    for part in range(2):
        axis = order[part][0]
        for d in range(1, 4):
            to = peer(me, axis, d)
            copies.append(send(snd1.at[pl.ds(part * 96 + to[axis] * N1, N1)], recv1.at[part, d - 1], to))
    exchange(copies)
    for part in range(2):
        mine = part * 96 + me[order[part][0]] * N1

        def add1(i, part=part, mine=mine):
            at = pl.ds(i * 6, 6)
            total = acc[pl.ds(mine + i * 6, 6)]
            for d in range(3):
                total = total + recv1[part, d, at].astype(F32)
            acc1[part, at] = total

        loop(4, add1)
    copies = []
    for part in range(2):
        axis = order[part][1]
        for d in range(1, 4):
            to = peer(me, axis, d)
            copies.append(send(acc1.at[part, pl.ds(to[axis] * N2, N2)], recv2.at[part, d - 1], to))
    exchange(copies)
    for part in range(2):
        total = acc1[part, pl.ds(me[order[part][1]] * N2, N2)]
        for d in range(3):
            total = total + recv2[part, d]
        acc2[part] = total

    def zslice(z):
        return pl.ds((z % 4) // 2 * N3, N3), slice(None), pl.ds(pl.multiple_of((z % 2) * 128, 128), 128)

    copies = []
    for d in range(1, 8):
        to = peer(me, "z", d)
        copies.append(send(acc2.at[(to["z"] // 4, *zslice(to["z"]))], recv3.at[d - 1], to))
    exchange(copies)
    z = me["z"]
    total = acc2[(z // 4, *zslice(z))]
    for d in range(7):
        total = total + recv3[d]
    part = z // 4
    first = (me["x"] * (1 - part) + me["y"] * part) * N1
    second = (me["y"] * (1 - part) + me["x"] * part) * N2
    base = c * N0 + part * 96 + first + second
    rows, _, lanes = zslice(z)
    shard = (pl.ds(base + (z % 4) // 2 * N3, N3), slice(None), lanes)
    full[shard] = total.astype(BF16)
    exchange([send(full.at[shard], full.at[shard], peer(me, "z", d)) for d in range(1, 8)])
    copies = []
    for part in range(2):
        a, b = order[part]
        at = pl.ds(c * N0 + part * 96 + me[a] * N1 + me[b] * N2, N2)
        for d in range(1, 4):
            copies.append(send(full.at[at], full.at[at], peer(me, b, d)))
    exchange(copies)
    copies = []
    for part in range(2):
        a, b = order[part]
        at = pl.ds(c * N0 + part * 96 + me[a] * N1, N1)
        for d in range(1, 4):
            copies.append(send(full.at[at], full.at[at], peer(me, a, d)))
    exchange(copies)
    at = pl.ds(c * N0, N0)
    exchange([send(full.at[at], full.at[at], peer(me, "c", 1))])

    def spread(i):
        s_out[pl.ds(i * 12, 12)] = full[pl.ds(i * 12, 12)].astype(F32)

    def spread_t(i):
        t_out[pl.ds(i * 12, 12)] = full[pl.ds(288 + i * 12, 12)].astype(F32)

    loop(24, spread)
    loop(8, spread_t)
    for copy in started:
        copy.wait_send()


def all_reduce(x):
    return pl.pallas_call(
        ar_kernel,
        out_shape=(jax.ShapeDtypeStruct((288, 8, 256), F32), jax.ShapeDtypeStruct((96, 8, 256), F32)),
        in_specs=[pl.BlockSpec(memory_space=pltpu.VMEM)],
        out_specs=(pl.BlockSpec(memory_space=pltpu.VMEM), pl.BlockSpec(memory_space=pltpu.VMEM)),
        scratch_shapes=AR_SCRATCH,
        compiler_params=pltpu.CompilerParams(
            collective_id=0, has_side_effects=True, vmem_limit_bytes=40 << 20
        ),
        name="all_reduce",
    )(x)


def extended(block, sides, width):
    for axis, dim in sides:
        count = lax.axis_size(axis)
        forward = [(i, i + 1) for i in range(count - 1)]
        backward = [(target, source) for source, target in forward]
        low = lax.ppermute(
            lax.slice_in_dim(block, block.shape[dim] - width, None, axis=dim), axis, forward
        )
        high = lax.ppermute(lax.slice_in_dim(block, 0, width, axis=dim), axis, backward)
        block = jnp.concatenate([low, block, high], axis=dim)
    return block


def shifted(block, axis, distance):
    devices = range(lax.axis_size(axis))
    route = [(i - distance, i) for i in devices if i - distance in devices]
    return lax.ppermute(block, axis, route)


def spatial_apply(padded, weights, rows, cols):
    chan = weights.shape[-1]
    total = jnp.zeros((padded.shape[0] * rows * cols, chan), jnp.float32)
    for i in range(3):
        for j in range(3):
            piece = padded[:, i : i + rows, j : j + cols, :].reshape(-1, chan)
            total = total + jnp.dot(piece, weights[i, j], preferred_element_type=jnp.float32)
    return total


def on_device(low_frames, spatial_weight, temporal_weight, cotangent):
    low = low_frames[0]
    grad_out = cotangent[0]
    frames, rows_low, cols_low, chan = low.shape
    rows = 2 * rows_low
    cols = 2 * cols_low
    low_ext = extended(low, (("height", 1),), 1)
    upsampled = jnp.repeat(jnp.repeat(low_ext, 2, axis=1), 2, axis=2)[:, 1:-1]
    padded = jnp.pad(upsampled, ((0, 0), (0, 0), (1, 1), (0, 0)))
    pre = spatial_apply(padded, spatial_weight, rows, cols)
    act = jax.nn.silu(pre).astype(jnp.bfloat16).reshape(frames, rows, cols, chan)
    earlier = shifted(act[frames - 2 :], "tm", 1)
    act_ext = jnp.concatenate([earlier, act], 0)
    mixed = padded[:, 1:-1, 1:-1, :].reshape(-1, chan).astype(jnp.float32)
    for k in range(3):
        mixed = mixed + jnp.dot(
            act_ext[2 - k : 2 - k + frames].reshape(-1, chan),
            temporal_weight[k],
            preferred_element_type=jnp.float32,
        )
    section_out = mixed.astype(jnp.bfloat16).reshape(1, frames, rows, cols, chan)
    later = shifted(grad_out[:2], "tm", -1)
    grad_ext = jnp.concatenate([grad_out, later], 0)
    grad_flat = grad_out.reshape(-1, chan)
    act_grad = jnp.zeros((frames * rows * cols, chan), jnp.float32)
    tgrads = []
    for k in range(3):
        act_grad = act_grad + jnp.dot(
            grad_ext[k : k + frames].reshape(-1, chan),
            temporal_weight[k].T,
            preferred_element_type=jnp.float32,
        )
        tgrads.append(
            lax.dot_general(
                act_ext[2 - k : 2 - k + frames].reshape(-1, chan),
                grad_flat,
                (((0,), (0,)), ((), ())),
                preferred_element_type=jnp.float32,
            )
        )
    temporal_grad = jnp.stack(tgrads)
    sig = jax.nn.sigmoid(pre)
    pre_grad = (act_grad * (sig * (1.0 + pre * (1.0 - sig)))).astype(jnp.bfloat16)
    sgrads = []
    for i in range(3):
        for j in range(3):
            piece = padded[:, i : i + rows, j : j + cols, :].reshape(-1, chan)
            sgrads.append(
                lax.dot_general(
                    piece, pre_grad, (((0,), (0,)), ((), ())), preferred_element_type=jnp.float32
                )
            )
    spatial_grad = jnp.stack(sgrads).reshape(3, 3, chan, chan)
    grad_rows = extended(pre_grad.reshape(frames, rows, cols, chan), (("height", 1),), 1)
    grad_pad = jnp.pad(grad_rows, ((0, 0), (0, 0), (1, 1), (0, 0)))
    total = grad_flat.astype(jnp.float32)
    for i in range(3):
        for j in range(3):
            piece = grad_pad[:, 2 - i : 2 - i + rows, 2 - j : 2 - j + cols, :].reshape(-1, chan)
            total = total + jnp.dot(
                piece, spatial_weight[i, j].T, preferred_element_type=jnp.float32
            )
    input_grad = (
        total.reshape(frames, rows_low, 2, cols_low, 2, chan).sum(axis=(2, 4)).astype(jnp.bfloat16)
    )
    both = jnp.concatenate([spatial_grad.reshape(9, chan, chan), temporal_grad], 0)
    spatial_grad, temporal_grad = all_reduce(both.reshape(384, 8, chan))
    spatial_grad = spatial_grad.reshape(3, 3, chan, chan)
    temporal_grad = temporal_grad.reshape(3, chan, chan)
    return (section_out, input_grad[None], spatial_grad, temporal_grad)


def solution(mesh):
    in_specs = (P("dp", "tm", "height", None, None), P(), P(), P("dp", "tm", "height", None, None))
    out_specs = (P("dp", "tm", "height", None, None), P("dp", "tm", "height", None, None), P(), P())
    return jax.shard_map(
        on_device, mesh=mesh, in_specs=in_specs, out_specs=out_specs, check_vma=False
    )
```

```python
import jax
import jax.numpy as jnp
from jax import lax
from jax.experimental import pallas as pl
from jax.experimental.pallas import tpu as pltpu
from jax.sharding import PartitionSpec as P

F32 = jnp.float32
BF16 = jnp.bfloat16
MESH = pl.DeviceIdType.MESH
N0, N1, N2, N3 = 192, 24, 6, 3
SIZE = dict(x=4, y=4, z=8, c=2)


def place():
    dp, tm, h = lax.axis_index("dp"), lax.axis_index("tm"), lax.axis_index("height")
    return dict(x=tm, y=dp // 2, z=(dp % 2) * 4 + h // 2, c=h % 2)


def device(p):
    return (p["y"] * 2 + p["z"] // 4, p["x"], (p["z"] % 4) * 2 + p["c"])


def peer(me, axis, d):
    return {**me, axis: (me[axis] + d) % SIZE[axis]}


def loop(count, body):
    def step(i, carry):
        body(i)
        return carry

    lax.fori_loop(0, count, step, 0)


def nn(a, b):
    return lax.dot_general(a, b, (((1,), (0,)), ((), ())), preferred_element_type=F32)


def nt(a, b):
    return lax.dot_general(a, b, (((1,), (1,)), ((), ())), preferred_element_type=F32)


SCRATCH = dict(
    wv=pltpu.VMEM((9, 256, 256), BF16),
    tv=pltpu.VMEM((3, 256, 256), BF16),
    low=pltpu.VMEM((6, 6, 32, 256), BF16),
    cot=pltpu.VMEM((6, 8, 64, 256), BF16),
    cotp=pltpu.VMEM((6, 512, 256), BF16),
    tmp=pltpu.VMEM((16, 64, 128), F32),
    ys=pltpu.VMEM((9, 24, 32, 256), F32),
    act=pltpu.VMEM((6, 512, 256), BF16),
    actT=pltpu.VMEM((4, 256, 512), BF16),
    lowT0=pltpu.VMEM((256, 640), BF16),
    lowT1=pltpu.VMEM((256, 512), BF16),
    lowT2=pltpu.VMEM((256, 640), BF16),
    ds=pltpu.VMEM((4, 512, 256), F32),
    pg=pltpu.VMEM((4, 10, 64, 256), BF16),
    odd=pltpu.VMEM((3, 4, 5, 32, 256), BF16),
    even=pltpu.VMEM((3, 4, 4, 32, 256), BF16),
    grads=pltpu.VMEM((384, 8, 256), F32),
    so_v=pltpu.VMEM((4, 8, 64, 256), BF16),
    ig_acc=pltpu.VMEM((512, 256), F32),
    ig_v=pltpu.VMEM((4, 4, 32, 256), BF16),
    fin=pltpu.VMEM((384, 8, 256), F32),
    recv0=pltpu.VMEM((N0, 8, 256), F32),
    acc=pltpu.VMEM((N0, 8, 256), F32),
    snd1=pltpu.VMEM((N0, 8, 256), BF16),
    recv1=pltpu.VMEM((2, 3, N1, 8, 256), BF16),
    acc1=pltpu.VMEM((2, N1, 8, 256), F32),
    recv2=pltpu.VMEM((2, 3, N2, 8, 256), F32),
    acc2=pltpu.VMEM((2, N2, 8, 256), F32),
    recv3=pltpu.VMEM((7, N3, 8, 128), F32),
    full=pltpu.VMEM((2 * N0, 8, 256), BF16),
    ssem=pltpu.SemaphoreType.DMA((49,)),
    rsem=pltpu.SemaphoreType.DMA((49,)),
    lsem=pltpu.SemaphoreType.DMA((24,)),
)


def kernel(low_hbm, w_hbm, t_hbm, cot_hbm, so_hbm, ig_hbm, s_hbm, tg_hbm, *scratch):
    s = dict(zip(SCRATCH, scratch))
    low, cot, cotp, ys, act, ds, pg = (s[n] for n in ("low", "cot", "cotp", "ys", "act", "ds", "pg"))
    odd, even, grads, tmp, full = (s[n] for n in ("odd", "even", "grads", "tmp", "full"))
    wv, tv = s["wv"], s["tv"]
    me = place()
    dp, tm, h = lax.axis_index("dp"), lax.axis_index("tm"), lax.axis_index("height")
    yes = True
    barrier = pltpu.get_barrier_semaphore()
    others = [device(peer(me, axis, d)) for axis in ("c", "x", "y", "z") for d in range(1, SIZE[axis])]
    others += [(dp, (tm + i) % 4, (h + j) % 8) for i in (0, 1, 3) for j in (1, 7)]
    for to in others:
        pl.semaphore_signal(barrier, inc=1, device_id=to, device_id_type=MESH)

    local_used = [0]

    def local(src, dst):
        copy = pltpu.make_async_copy(src, dst, s["lsem"].at[local_used[0]])
        local_used[0] += 1
        copy.start()
        return copy

    load_low = local(low_hbm, low.at[pl.ds(2, 4), pl.ds(1, 4)])
    load_w = local(w_hbm, wv)
    load_cot = local(cot_hbm, cot.at[pl.ds(0, 4)])
    load_t = local(t_hbm, tv)

    @pl.when(tm == 0)
    def _():
        low[0:2] = jnp.zeros((2, 6, 32, 256), BF16)

    @pl.when(tm == 3)
    def _():
        cot[4:6] = jnp.zeros((2, 8, 64, 256), BF16)

    @pl.when(h == 0)
    def _():
        low[2:6, 0] = jnp.zeros((4, 32, 256), BF16)
        pg[:, 0] = jnp.zeros((4, 64, 256), BF16)

    @pl.when(h == 7)
    def _():
        low[2:6, 5] = jnp.zeros((4, 32, 256), BF16)
        pg[:, 9] = jnp.zeros((4, 64, 256), BF16)

    @pl.when((h == 0) & (tm > 0))
    def _():
        low[0:2, 0] = jnp.zeros((2, 32, 256), BF16)

    @pl.when((h == 7) & (tm > 0))
    def _():
        low[0:2, 5] = jnp.zeros((2, 32, 256), BF16)

    pl.semaphore_wait(barrier, len(others))
    used = [0]
    halos = []

    def halo(src, dst, to, sends, receives):
        k = used[0]
        used[0] += 1
        copy = pltpu.make_async_remote_copy(
            src_ref=src, dst_ref=dst, send_sem=s["ssem"].at[k], recv_sem=s["rsem"].at[k],
            device_id=to, device_id_type=MESH,
        )

        @pl.when(sends)
        def _():
            copy.start()

        halos.append((copy, sends))
        return copy, receives

    def arrive(pair):
        copy, receives = pair

        @pl.when(receives)
        def _():
            copy.wait_recv()

    up, down, right, left = (h + 1) % 8, (h + 7) % 8, (tm + 1) % 4, (tm + 3) % 4
    own, early = pl.ds(2, 4), pl.ds(0, 2)
    low_up = halo(low_hbm.at[:, 3], low.at[own, 0], (dp, tm, up), h < 7, h > 0)
    low_down = halo(low_hbm.at[:, 0], low.at[own, 5], (dp, tm, down), h > 0, h < 7)
    cots = [
        halo(cot_hbm.at[f], cot.at[4 + f], (dp, left, h), tm > 0, tm < 3) for f in range(2)
    ]
    last = pl.ds(2, 2)
    early_low = [
        halo(low_hbm.at[last], low.at[early, pl.ds(1, 4)], (dp, right, h), tm < 3, tm > 0),
        halo(low_hbm.at[last, 3], low.at[early, 0], (dp, right, up), (tm < 3) & (h < 7), (tm > 0) & (h > 0)),
        halo(low_hbm.at[last, 0], low.at[early, 5], (dp, right, down), (tm < 3) & (h > 0), (tm > 0) & (h < 7)),
    ]

    def split_columns(f):
        def row(y):
            for half in range(2):
                lanes = pl.ds(half * 128, 128)
                tmp[y * 2 + half] = cot[f, y, :, lanes].astype(F32)
                for b in range(2):
                    part = tmp[y * 2 + half, pl.ds(b, 32, stride=2), :]
                    cotp[f, pl.ds(y * 64 + b * 32, 32), lanes] = part.astype(BF16)

        loop(8, row)

    load_cot.wait()
    loop(4, split_columns)
    load_low.wait()
    load_w.wait()
    load_t.wait()
    arrive(low_up)
    arrive(low_down)
    col = lax.broadcasted_iota(jnp.int32, (32, 256), 0)

    def from_left(v):
        return jnp.where(col == 0, 0.0, pltpu.roll(v, 1, 0))

    def from_right(v):
        return jnp.where(col == 31, 0.0, pltpu.roll(v, 31, 0))

    def products(first, count):
        def one(ij):
            rows = low[pl.ds(first, count)].reshape(count * 192, 256)
            ys[ij, 0 : count * 6] = nn(rows, wv[ij]).reshape(count * 6, 32, 256)

        loop(9, one)

    def activate(first, count, slopes):
        def one(n):
            f, r = n // 4, n % 4
            at = f * 6 + r + 1
            for a in range(2):
                z = [ys[j, at - 1 + a] + ys[3 + j, at] + ys[6 + j, at + a] for j in range(3)]
                pres = (from_left(z[0]) + z[1] + z[2], z[0] + z[1] + from_right(z[2]))
                for b in range(2):
                    pre = pres[b]
                    sig = jax.nn.sigmoid(pre)
                    tokens = pl.ds((r * 2 + a) * 64 + b * 32, 32)
                    act[first + f, tokens] = (pre * sig).astype(BF16)
                    if slopes:
                        ds[f, tokens] = sig * (1.0 + pre * (1.0 - sig))

        loop(count * 4, one)

    products(2, 4)
    activate(2, 4, True)

    def flip(f):
        s["actT"][f] = act[2 + f].T

    loop(4, flip)
    s["lowT0"][...] = low[2:6, 0:5].reshape(640, 256).T
    s["lowT1"][...] = low[2:6, 1:5].reshape(512, 256).T
    s["lowT2"][...] = low[2:6, 1:6].reshape(640, 256).T

    def pre_grad(f):
        total = nt(cotp[f], tv[0]) + nt(cotp[f + 1], tv[1]) + nt(cotp[f + 2], tv[2])
        pg[f, 1:9] = (total * ds[f]).astype(BF16).reshape(8, 64, 256)

    loop(2, pre_grad)
    for pair in early_low:
        arrive(pair)
    products(0, 2)
    activate(0, 2, False)
    outs = []

    def section(t):
        total = nn(act[t + 2], tv[0]) + nn(act[t + 1], tv[1]) + nn(act[t], tv[2])
        for y in range(8):
            up_row = low[t + 2, y // 2 + 1].astype(F32)
            for b in range(2):
                at = y * 64 + b * 32
                value = total[at : at + 32] + up_row
                for half in range(2):
                    tmp[y * 2 + half, pl.ds(b, 32, stride=2), :] = value[:, half * 128 : half * 128 + 128]
        for y in range(8):
            for half in range(2):
                s["so_v"][t, y, :, half * 128 : half * 128 + 128] = tmp[y * 2 + half].astype(BF16)

    loop(4, section)
    outs.append(local(s["so_v"], so_hbm))

    for f in range(2):
        arrive(cots[f])
        split_columns(4 + f)
        pre_grad(2 + f)
    pg_up = halo(pg.at[:, 8], pg.at[:, 0], (dp, tm, up), h < 7, h > 0)
    pg_down = halo(pg.at[:, 1], pg.at[:, 9], (dp, tm, down), h > 0, h < 7)

    for k in range(3):
        total = nn(s["actT"][0], cotp[k])
        for f in range(1, 4):
            total = total + nn(s["actT"][f], cotp[f + k])
        grads[288 + 32 * k : 320 + 32 * k] = total.reshape(32, 8, 256)

    def put(ref, f, q, even_cols, odd_cols):
        ref[0, f, q] = (odd_cols + from_right(even_cols)).astype(BF16)
        ref[1, f, q] = (odd_cols + even_cols).astype(BF16)
        ref[2, f, q] = (from_left(odd_cols) + even_cols).astype(BF16)

    def rows_of(f, slots):
        halves = []
        for b in range(2):
            total = pg[f, slots[0], b * 32 : b * 32 + 32].astype(F32)
            for slot in slots[1:]:
                total = total + pg[f, slot, b * 32 : b * 32 + 32].astype(F32)
            halves.append(total)
        return halves

    def box(f):
        for q in range(5):
            slots = [n for n in (2 * q, 2 * q + 1) if 0 < n < 9]
            put(odd, f, q, *rows_of(f, slots))
        for r in range(4):
            put(even, f, r, *rows_of(f, (2 * r + 1, 2 * r + 2)))

    loop(4, box)

    def weight_grads(j):
        sums = odd[j].reshape(640, 256)
        grads[pl.ds(j * 32, 32)] = nn(s["lowT0"][...], sums).reshape(32, 8, 256)
        grads[pl.ds((6 + j) * 32, 32)] = nn(s["lowT2"][...], sums).reshape(32, 8, 256)
        grads[pl.ds((3 + j) * 32, 32)] = nn(s["lowT1"][...], even[j].reshape(512, 256)).reshape(32, 8, 256)

    loop(3, weight_grads)

    started = []

    def send(src, dst, to):
        k = used[0]
        used[0] += 1
        copy = pltpu.make_async_remote_copy(
            src_ref=src, dst_ref=dst, send_sem=s["ssem"].at[k], recv_sem=s["rsem"].at[k],
            device_id=device(to), device_id_type=MESH,
        )
        copy.start()
        started.append(copy)
        return copy

    def wait(copies):
        for copy in copies:
            copy.wait_recv()

    c = me["c"]
    recv0, acc, snd1, recv1, acc1, recv2, acc2, recv3 = (
        s[n] for n in ("recv0", "acc", "snd1", "recv1", "acc1", "recv2", "acc2", "recv3")
    )
    copies = [send(grads.at[pl.ds((1 - c) * N0, N0)], recv0, peer(me, "c", 1))]

    arrive(pg_up)
    arrive(pg_down)

    def edge(f):
        put(odd, f, 0, *rows_of(f, (0, 1)))
        put(odd, f, 4, *rows_of(f, (8, 9)))

    loop(4, edge)

    def cot_sum(n):
        f, r = n // 4, n % 4
        total = jnp.zeros((32, 256), F32)
        for q in range(4):
            total = total + cotp[f, pl.ds(r * 128 + q * 32, 32)].astype(F32)
        s["ig_acc"][pl.ds(n * 32, 32)] = total

    loop(16, cot_sum)

    wait(copies)

    def add0(i):
        at = pl.ds(i * 12, 12)
        total = grads[pl.ds(c * N0 + i * 12, 12)] + recv0[at]
        acc[at] = total
        snd1[at] = total.astype(BF16)

    loop(16, add0)
    order = (("x", "y"), ("y", "x"))
    copies = []
    for part in range(2):
        axis = order[part][0]
        for d in range(1, 4):
            to = peer(me, axis, d)
            copies.append(send(snd1.at[pl.ds(part * 96 + to[axis] * N1, N1)], recv1.at[part, d - 1], to))

    def inputs(j):
        total = nt(odd[j, :, 1:5].reshape(512, 256), wv[j])
        total = total + nt(even[j].reshape(512, 256), wv[3 + j])
        total = total + nt(odd[j, :, 0:4].reshape(512, 256), wv[6 + j])
        s["ig_acc"][...] += total

    loop(3, inputs)
    s["ig_v"][...] = s["ig_acc"][...].astype(BF16).reshape(4, 4, 32, 256)
    outs.append(local(s["ig_v"], ig_hbm))

    wait(copies)
    for part in range(2):
        mine = part * 96 + me[order[part][0]] * N1

        def add1(i, part=part, mine=mine):
            at = pl.ds(i * 6, 6)
            total = acc[pl.ds(mine + i * 6, 6)]
            for d in range(3):
                total = total + recv1[part, d, at].astype(F32)
            acc1[part, at] = total

        loop(4, add1)
    copies = []
    for part in range(2):
        axis = order[part][1]
        for d in range(1, 4):
            to = peer(me, axis, d)
            copies.append(send(acc1.at[part, pl.ds(to[axis] * N2, N2)], recv2.at[part, d - 1], to))
    wait(copies)
    for part in range(2):
        total = acc1[part, pl.ds(me[order[part][1]] * N2, N2)]
        for d in range(3):
            total = total + recv2[part, d]
        acc2[part] = total

    def zslice(z):
        return pl.ds((z % 4) // 2 * N3, N3), slice(None), pl.ds(pl.multiple_of((z % 2) * 128, 128), 128)

    copies = []
    for d in range(1, 8):
        to = peer(me, "z", d)
        copies.append(send(acc2.at[(to["z"] // 4, *zslice(to["z"]))], recv3.at[d - 1], to))
    wait(copies)
    z = me["z"]
    total = acc2[(z // 4, *zslice(z))]
    for d in range(7):
        total = total + recv3[d]
    part = z // 4
    first = (me["x"] * (1 - part) + me["y"] * part) * N1
    second = (me["y"] * (1 - part) + me["x"] * part) * N2
    base = c * N0 + part * 96 + first + second
    lanes = zslice(z)[2]
    shard = (pl.ds(base + (z % 4) // 2 * N3, N3), slice(None), lanes)
    full[shard] = total.astype(BF16)
    wait([send(full.at[shard], full.at[shard], peer(me, "z", d)) for d in range(1, 8)])
    copies = []
    for part in range(2):
        a, b = order[part]
        at = pl.ds(c * N0 + part * 96 + me[a] * N1 + me[b] * N2, N2)
        for d in range(1, 4):
            copies.append(send(full.at[at], full.at[at], peer(me, b, d)))
    wait(copies)
    copies = []
    for part in range(2):
        a, b = order[part]
        at = pl.ds(c * N0 + part * 96 + me[a] * N1, N1)
        for d in range(1, 4):
            copies.append(send(full.at[at], full.at[at], peer(me, a, d)))
    wait(copies)
    at = pl.ds(c * N0, N0)
    copies = [send(full.at[at], full.at[at], peer(me, "c", 1))]
    fin = s["fin"]

    def spread(first):
        def one(i):
            fin[pl.ds(first + i * 12, 12)] = full[pl.ds(first + i * 12, 12)].astype(F32)

        loop(16, one)

    spread(c * N0)
    wait(copies)
    spread((1 - c) * N0)
    outs.append(local(fin.at[pl.ds(0, 288)], s_hbm))
    outs.append(local(fin.at[pl.ds(288, 96)], tg_hbm))
    for copy in started:
        copy.wait_send()
    for copy, sends in halos:

        @pl.when(sends)
        def _(copy=copy):
            copy.wait_send()

    for copy in outs:
        copy.wait()


def on_device(low_frames, spatial_weight, temporal_weight, cotangent):
    any_space = pl.BlockSpec(memory_space=pl.ANY)
    outs = pl.pallas_call(
        kernel,
        out_shape=(
            jax.ShapeDtypeStruct((4, 8, 64, 256), BF16),
            jax.ShapeDtypeStruct((4, 4, 32, 256), BF16),
            jax.ShapeDtypeStruct((288, 8, 256), F32),
            jax.ShapeDtypeStruct((96, 8, 256), F32),
        ),
        in_specs=[any_space] * 4,
        out_specs=(any_space,) * 4,
        scratch_shapes=list(SCRATCH.values()),
        compiler_params=pltpu.CompilerParams(
            collective_id=0, has_side_effects=True, vmem_limit_bytes=60 << 20
        ),
        name="section",
    )(low_frames[0], spatial_weight.reshape(9, 256, 256), temporal_weight, cotangent[0])
    section_out, input_grad, spatial_grad, temporal_grad = outs
    return (
        section_out[None],
        input_grad[None],
        spatial_grad.reshape(3, 3, 256, 256),
        temporal_grad.reshape(3, 256, 256),
    )


def solution(mesh):
    in_specs = (P("dp", "tm", "height", None, None), P(), P(), P("dp", "tm", "height", None, None))
    out_specs = (P("dp", "tm", "height", None, None), P("dp", "tm", "height", None, None), P(), P())
    return jax.shard_map(
        on_device, mesh=mesh, in_specs=in_specs, out_specs=out_specs, check_vma=False
    )
```

```python
import jax
import jax.numpy as jnp
from jax import lax
from jax.experimental import pallas as pl
from jax.experimental.pallas import tpu as pltpu
from jax.sharding import PartitionSpec as P

F32 = jnp.float32
BF16 = jnp.bfloat16
MESH = pl.DeviceIdType.MESH
CHUNKS = 3
N0, N1, N2, N3 = 64, 8, 2, 1
HALF = N0 // 2
PLACES = (9, 10, 11, 3, 0, 6, 1, 7, 4, 5, 2, 8)
SLOT = [PLACES.index(m) for m in range(12)]
SIZE = dict(x=4, y=4, z=8, c=2)


def place():
    dp, tm, h = lax.axis_index("dp"), lax.axis_index("tm"), lax.axis_index("height")
    return dict(x=tm, y=dp // 2, z=(dp % 2) * 4 + h // 2, c=h % 2)


def device(p):
    return (p["y"] * 2 + p["z"] // 4, p["x"], (p["z"] % 4) * 2 + p["c"])


def peer(me, axis, d):
    return {**me, axis: (me[axis] + d) % SIZE[axis]}


def loop(count, body):
    def step(i, carry):
        body(i)
        return carry

    lax.fori_loop(0, count, step, 0)


def nn(a, b):
    return lax.dot_general(a, b, (((1,), (0,)), ((), ())), preferred_element_type=F32)


def nt(a, b):
    return lax.dot_general(a, b, (((1,), (1,)), ((), ())), preferred_element_type=F32)


SCRATCH = dict(
    wv=pltpu.VMEM((9, 256, 256), BF16),
    tv=pltpu.VMEM((3, 256, 256), BF16),
    low=pltpu.VMEM((6, 6, 32, 256), BF16),
    cot=pltpu.VMEM((6, 8, 64, 256), BF16),
    cotp=pltpu.VMEM((6, 512, 256), BF16),
    tmp=pltpu.VMEM((16, 64, 128), F32),
    ys=pltpu.VMEM((9, 24, 32, 256), F32),
    act=pltpu.VMEM((6, 512, 256), BF16),
    actT=pltpu.VMEM((4, 256, 512), BF16),
    lowT0=pltpu.VMEM((256, 640), BF16),
    lowT1=pltpu.VMEM((256, 512), BF16),
    lowT2=pltpu.VMEM((256, 640), BF16),
    ds=pltpu.VMEM((4, 512, 256), F32),
    pg=pltpu.VMEM((4, 10, 64, 256), BF16),
    odd=pltpu.VMEM((3, 4, 5, 32, 256), BF16),
    even=pltpu.VMEM((3, 4, 4, 32, 256), BF16),
    grads=pltpu.VMEM((384, 8, 256), F32),
    ig_acc=pltpu.VMEM((512, 256), F32),
    recv0=pltpu.VMEM((CHUNKS, N0, 8, 256), F32),
    acc=pltpu.VMEM((CHUNKS, N0, 8, 256), F32),
    snd1=pltpu.VMEM((CHUNKS, N0, 8, 256), BF16),
    recv1=pltpu.VMEM((CHUNKS, 2, 3, N1, 8, 256), BF16),
    acc1=pltpu.VMEM((CHUNKS, 2, N1, 8, 256), F32),
    recv2=pltpu.VMEM((CHUNKS, 2, 3, N2, 8, 256), F32),
    acc2=pltpu.VMEM((CHUNKS, 2, N2, 8, 256), F32),
    recv3=pltpu.VMEM((CHUNKS, 7, N3, 8, 128), F32),
    full=pltpu.VMEM((CHUNKS * 2 * N0, 8, 256), BF16),
    ssem=pltpu.SemaphoreType.DMA((9 + 40 * CHUNKS,)),
    rsem=pltpu.SemaphoreType.DMA((9 + 40 * CHUNKS,)),
    lsem=pltpu.SemaphoreType.DMA((24,)),
)


def kernel(low_hbm, w_hbm, t_hbm, cot_hbm, so_v, ig_v, s_v, tg_v, *scratch):
    s = dict(zip(SCRATCH, scratch))
    low, cot, cotp, ys, act, ds, pg = (s[n] for n in ("low", "cot", "cotp", "ys", "act", "ds", "pg"))
    odd, even, grads, tmp, full = (s[n] for n in ("odd", "even", "grads", "tmp", "full"))
    wv, tv = s["wv"], s["tv"]
    me = place()
    dp, tm, h = lax.axis_index("dp"), lax.axis_index("tm"), lax.axis_index("height")
    yes = True
    barrier = pltpu.get_barrier_semaphore()
    others = [device(peer(me, axis, d)) for axis in ("c", "x", "y", "z") for d in range(1, SIZE[axis])]
    others += [(dp, (tm + i) % 4, (h + j) % 8) for i in (0, 1, 3) for j in (1, 7)]
    for to in others:
        pl.semaphore_signal(barrier, inc=1, device_id=to, device_id_type=MESH)

    local_used = [0]

    def local(src, dst):
        copy = pltpu.make_async_copy(src, dst, s["lsem"].at[local_used[0]])
        local_used[0] += 1
        copy.start()
        return copy

    load_low = local(low_hbm, low.at[pl.ds(2, 4), pl.ds(1, 4)])
    load_w = local(w_hbm, wv)
    load_cot = local(cot_hbm, cot.at[pl.ds(0, 4)])
    load_t = local(t_hbm, tv)

    @pl.when(tm == 0)
    def _():
        low[0:2] = jnp.zeros((2, 6, 32, 256), BF16)

    @pl.when(tm == 3)
    def _():
        cot[4:6] = jnp.zeros((2, 8, 64, 256), BF16)

    @pl.when(h == 0)
    def _():
        low[2:6, 0] = jnp.zeros((4, 32, 256), BF16)
        pg[:, 0] = jnp.zeros((4, 64, 256), BF16)

    @pl.when(h == 7)
    def _():
        low[2:6, 5] = jnp.zeros((4, 32, 256), BF16)
        pg[:, 9] = jnp.zeros((4, 64, 256), BF16)

    @pl.when((h == 0) & (tm > 0))
    def _():
        low[0:2, 0] = jnp.zeros((2, 32, 256), BF16)

    @pl.when((h == 7) & (tm > 0))
    def _():
        low[0:2, 5] = jnp.zeros((2, 32, 256), BF16)

    pl.semaphore_wait(barrier, len(others))
    used = [0]
    halos = []

    def halo(src, dst, to, sends, receives):
        k = used[0]
        used[0] += 1
        copy = pltpu.make_async_remote_copy(
            src_ref=src, dst_ref=dst, send_sem=s["ssem"].at[k], recv_sem=s["rsem"].at[k],
            device_id=to, device_id_type=MESH,
        )

        @pl.when(sends)
        def _():
            copy.start()

        halos.append((copy, sends))
        return copy, receives

    def arrive(pair):
        copy, receives = pair

        @pl.when(receives)
        def _():
            copy.wait_recv()

    up, down, right, left = (h + 1) % 8, (h + 7) % 8, (tm + 1) % 4, (tm + 3) % 4
    own, early = pl.ds(2, 4), pl.ds(0, 2)
    low_up = halo(low_hbm.at[:, 3], low.at[own, 0], (dp, tm, up), h < 7, h > 0)
    low_down = halo(low_hbm.at[:, 0], low.at[own, 5], (dp, tm, down), h > 0, h < 7)
    cots = [
        halo(cot_hbm.at[f], cot.at[4 + f], (dp, left, h), tm > 0, tm < 3) for f in range(2)
    ]
    last = pl.ds(2, 2)
    early_low = [
        halo(low_hbm.at[last], low.at[early, pl.ds(1, 4)], (dp, right, h), tm < 3, tm > 0),
        halo(low_hbm.at[last, 3], low.at[early, 0], (dp, right, up), (tm < 3) & (h < 7), (tm > 0) & (h > 0)),
        halo(low_hbm.at[last, 0], low.at[early, 5], (dp, right, down), (tm < 3) & (h > 0), (tm > 0) & (h < 7)),
    ]

    def split_columns(f):
        def row(y):
            for half in range(2):
                lanes = pl.ds(half * 128, 128)
                tmp[y * 2 + half] = cot[f, y, :, lanes].astype(F32)
                for b in range(2):
                    part = tmp[y * 2 + half, pl.ds(b, 32, stride=2), :]
                    cotp[f, pl.ds(y * 64 + b * 32, 32), lanes] = part.astype(BF16)

        loop(8, row)

    load_cot.wait()
    loop(4, split_columns)
    load_low.wait()
    load_w.wait()
    load_t.wait()
    arrive(low_up)
    arrive(low_down)
    col = lax.broadcasted_iota(jnp.int32, (32, 256), 0)

    def from_left(v):
        return jnp.where(col == 0, 0.0, pltpu.roll(v, 1, 0))

    def from_right(v):
        return jnp.where(col == 31, 0.0, pltpu.roll(v, 31, 0))

    def products(first, count):
        def one(ij):
            rows = low[pl.ds(first, count)].reshape(count * 192, 256)
            ys[ij, 0 : count * 6] = nn(rows, wv[ij]).reshape(count * 6, 32, 256)

        loop(9, one)

    def activate(first, count, slopes):
        def one(n):
            f, r = n // 4, n % 4
            at = f * 6 + r + 1
            for a in range(2):
                z = [ys[j, at - 1 + a] + ys[3 + j, at] + ys[6 + j, at + a] for j in range(3)]
                pres = (from_left(z[0]) + z[1] + z[2], z[0] + z[1] + from_right(z[2]))
                for b in range(2):
                    pre = pres[b]
                    sig = jax.nn.sigmoid(pre)
                    tokens = pl.ds((r * 2 + a) * 64 + b * 32, 32)
                    act[first + f, tokens] = (pre * sig).astype(BF16)
                    if slopes:
                        ds[f, tokens] = sig * (1.0 + pre * (1.0 - sig))

        loop(count * 4, one)

    products(2, 4)
    activate(2, 4, True)

    def flip(f):
        s["actT"][f] = act[2 + f].T

    loop(4, flip)
    s["lowT0"][...] = low[2:6, 0:5].reshape(640, 256).T
    s["lowT1"][...] = low[2:6, 1:5].reshape(512, 256).T
    s["lowT2"][...] = low[2:6, 1:6].reshape(640, 256).T

    def pre_grad(f):
        total = nt(cotp[f], tv[0]) + nt(cotp[f + 1], tv[1]) + nt(cotp[f + 2], tv[2])
        pg[f, 1:9] = (total * ds[f]).astype(BF16).reshape(8, 64, 256)

    loop(2, pre_grad)
    for pair in early_low:
        arrive(pair)
    products(0, 2)
    activate(0, 2, False)

    def section(t):
        total = nn(act[t + 2], tv[0]) + nn(act[t + 1], tv[1]) + nn(act[t], tv[2])
        for y in range(8):
            up_row = low[t + 2, y // 2 + 1].astype(F32)
            for b in range(2):
                at = y * 64 + b * 32
                value = total[at : at + 32] + up_row
                for half in range(2):
                    tmp[y * 2 + half, pl.ds(b, 32, stride=2), :] = value[:, half * 128 : half * 128 + 128]
        for y in range(8):
            for half in range(2):
                so_v[t, y, :, half * 128 : half * 128 + 128] = tmp[y * 2 + half].astype(BF16)

    loop(4, section)

    for f in range(2):
        arrive(cots[f])
        split_columns(4 + f)
        pre_grad(2 + f)
    pg_up = halo(pg.at[:, 8], pg.at[:, 0], (dp, tm, up), h < 7, h > 0)
    pg_down = halo(pg.at[:, 1], pg.at[:, 9], (dp, tm, down), h > 0, h < 7)

    for k in range(3):
        total = nn(s["actT"][0], cotp[k])
        for f in range(1, 4):
            total = total + nn(s["actT"][f], cotp[f + k])
        grads[32 * k : 32 * k + 32] = total.reshape(32, 8, 256)

    def put(ref, f, q, even_cols, odd_cols):
        ref[0, f, q] = (odd_cols + from_right(even_cols)).astype(BF16)
        ref[1, f, q] = (odd_cols + even_cols).astype(BF16)
        ref[2, f, q] = (from_left(odd_cols) + even_cols).astype(BF16)

    def rows_of(f, slots):
        halves = []
        for b in range(2):
            total = pg[f, slots[0], b * 32 : b * 32 + 32].astype(F32)
            for slot in slots[1:]:
                total = total + pg[f, slot, b * 32 : b * 32 + 32].astype(F32)
            halves.append(total)
        return halves

    def box(f):
        for q in range(5):
            slots = [n for n in (2 * q, 2 * q + 1) if 0 < n < 9]
            put(odd, f, q, *rows_of(f, slots))
        for r in range(4):
            put(even, f, r, *rows_of(f, (2 * r + 1, 2 * r + 2)))

    loop(4, box)

    started = []

    def send(src, dst, to):
        k = used[0]
        used[0] += 1
        copy = pltpu.make_async_remote_copy(
            src_ref=src, dst_ref=dst, send_sem=s["ssem"].at[k], recv_sem=s["rsem"].at[k],
            device_id=device(to), device_id_type=MESH,
        )
        copy.start()
        started.append(copy)
        return copy

    def weight_grad(m):
        i, j = m // 3, m % 3
        if i == 1:
            total = nn(s["lowT1"][...], even[j].reshape(512, 256))
        else:
            total = nn(s["lowT0" if i == 0 else "lowT2"][...], odd[j].reshape(640, 256))
        at = SLOT[m] * 32
        grads[at : at + 32] = total.reshape(32, 8, 256)

    c, z = me["c"], me["z"]
    order = (("x", "y"), ("y", "x"))
    recv0, acc, snd1, recv1, acc1, recv2, acc2, recv3 = (
        s[n] for n in ("recv0", "acc", "snd1", "recv1", "acc1", "recv2", "acc2", "recv3")
    )

    def base(k):
        return k * 2 * N0 + c * N0

    def zslice(to):
        return pl.ds((to % 4) // 2, N3), slice(None), pl.ds(pl.multiple_of((to % 2) * 128, 128), 128)

    def stage0(k):
        for m in PLACES[4 * k : 4 * k + 4]:
            if m < 9:
                weight_grad(m)
        return [send(grads.at[pl.ds(k * 2 * N0 + (1 - c) * N0, N0)], recv0.at[k], peer(me, "c", 1))]

    def stage1(k):
        def add(i):
            at = pl.ds(i * 8, 8)
            total = grads[pl.ds(base(k) + i * 8, 8)] + recv0[k, at]
            acc[k, at] = total
            snd1[k, at] = total.astype(BF16)

        loop(N0 // 8, add)
        copies = []
        for part in range(2):
            axis = order[part][0]
            for d in range(1, 4):
                to = peer(me, axis, d)
                src = snd1.at[k, pl.ds(part * HALF + to[axis] * N1, N1)]
                copies.append(send(src, recv1.at[k, part, d - 1], to))
        return copies

    def stage2(k):
        for part in range(2):
            total = acc[k, pl.ds(part * HALF + me[order[part][0]] * N1, N1)]
            for d in range(3):
                total = total + recv1[k, part, d].astype(F32)
            acc1[k, part] = total
        copies = []
        for part in range(2):
            axis = order[part][1]
            for d in range(1, 4):
                to = peer(me, axis, d)
                copies.append(send(acc1.at[k, part, pl.ds(to[axis] * N2, N2)], recv2.at[k, part, d - 1], to))
        return copies

    def stage3(k):
        for part in range(2):
            total = acc1[k, part, pl.ds(me[order[part][1]] * N2, N2)]
            for d in range(3):
                total = total + recv2[k, part, d]
            acc2[k, part] = total
        copies = []
        for d in range(1, 8):
            to = peer(me, "z", d)
            copies.append(send(acc2.at[(k, to["z"] // 4, *zslice(to["z"]))], recv3.at[k, d - 1], to))
        return copies

    def stage4(k):
        total = acc2[(k, z // 4, *zslice(z))]
        for d in range(7):
            total = total + recv3[k, d]
        part = z // 4
        first = (me["x"] * (1 - part) + me["y"] * part) * N1
        second = (me["y"] * (1 - part) + me["x"] * part) * N2
        at = base(k) + part * HALF + first + second + (z % 4) // 2
        shard = (pl.ds(at, N3), slice(None), zslice(z)[2])
        full[shard] = total.astype(BF16)
        return [send(full.at[shard], full.at[shard], peer(me, "z", d)) for d in range(1, 8)]

    def spread_by(k, depth):
        copies = []
        for part in range(2):
            a, b = order[part]
            if depth == 2:
                at, axis = pl.ds(base(k) + part * HALF + me[a] * N1 + me[b] * N2, N2), b
            else:
                at, axis = pl.ds(base(k) + part * HALF + me[a] * N1, N1), a
            copies += [send(full.at[at], full.at[at], peer(me, axis, d)) for d in range(1, 4)]
        return copies

    def stage5(k):
        return spread_by(k, 2)

    def stage6(k):
        return spread_by(k, 1)

    def stage7(k):
        at = pl.ds(base(k), N0)
        return [send(full.at[at], full.at[at], peer(me, "c", 1))]

    def stage8(k):
        for n in range(4 * k, 4 * k + 4):
            m = PLACES[n]
            ref, at = (s_v, m) if m < 9 else (tg_v, m - 9)

            def widen(i, n=n, ref=ref, at=at):
                ref[pl.ds(at * 32 + i * 8, 8)] = full[pl.ds(n * 32 + i * 8, 8)].astype(F32)

            loop(4, widen)
        return []

    def edge(f):
        put(odd, f, 0, *rows_of(f, (0, 1)))
        put(odd, f, 4, *rows_of(f, (8, 9)))

    def cot_sum(n):
        f, r = n // 4, n % 4
        total = jnp.zeros((32, 256), F32)
        for q in range(4):
            total = total + cotp[f, pl.ds(r * 128 + q * 32, 32)].astype(F32)
        s["ig_acc"][pl.ds(n * 32, 32)] = total

    def inputs(j):
        total = nt(odd[j, :, 1:5].reshape(512, 256), wv[j])
        total = total + nt(even[j].reshape(512, 256), wv[3 + j])
        total = total + nt(odd[j, :, 0:4].reshape(512, 256), wv[6 + j])
        s["ig_acc"][...] += total

    def input_grad():
        arrive(pg_up)
        arrive(pg_down)
        loop(4, edge)
        loop(16, cot_sum)
        loop(3, inputs)
        ig_v[...] = s["ig_acc"][...].astype(BF16).reshape(4, 4, 32, 256)

    stages = (stage0, stage1, stage2, stage3, stage4, stage5, stage6, stage7, stage8)
    flying = [[] for _ in range(CHUNKS)]
    for stage in stages:
        for k in range(CHUNKS):
            for copy in flying[k]:
                copy.wait_recv()
            flying[k] = stage(k)
        if stage is stage1:
            input_grad()
    for copy in started:
        copy.wait_send()
    for copy, sends in halos:

        @pl.when(sends)
        def _(copy=copy):
            copy.wait_send()


def store(so_v, ig_v, s_v, tg_v, so, ig, sg, tg, sems):
    copies = [
        pltpu.make_async_copy(src, dst, sems.at[n])
        for n, (src, dst) in enumerate(((so_v, so), (s_v, sg), (tg_v, tg), (ig_v, ig)))
    ]
    for copy in copies:
        copy.start()
    for copy in copies:
        copy.wait()


def on_device(low_frames, spatial_weight, temporal_weight, cotangent):
    hbm = pl.BlockSpec(memory_space=pltpu.HBM)
    vmem = pl.BlockSpec(memory_space=pltpu.VMEM)
    shapes = (
        jax.ShapeDtypeStruct((4, 8, 64, 256), BF16),
        jax.ShapeDtypeStruct((4, 4, 32, 256), BF16),
        jax.ShapeDtypeStruct((288, 8, 256), F32),
        jax.ShapeDtypeStruct((96, 8, 256), F32),
    )
    held = pl.pallas_call(
        kernel,
        out_shape=tuple(pltpu.VMEM(a.shape, a.dtype) for a in shapes),
        in_specs=[hbm] * 4,
        out_specs=(vmem,) * 4,
        scratch_shapes=list(SCRATCH.values()),
        compiler_params=pltpu.CompilerParams(
            collective_id=0, has_side_effects=True, vmem_limit_bytes=52 << 20
        ),
        name="section",
    )(low_frames[0], spatial_weight.reshape(9, 256, 256), temporal_weight, cotangent[0])
    outs = pl.pallas_call(
        store,
        out_shape=shapes,
        in_specs=[vmem] * 4,
        out_specs=(hbm,) * 4,
        scratch_shapes=[pltpu.SemaphoreType.DMA((4,))],
        compiler_params=pltpu.CompilerParams(vmem_limit_bytes=4 << 20),
        name="store",
    )(*(pltpu.with_memory_space_constraint(a, pltpu.VMEM) for a in held))
    section_out, input_grad, spatial_grad, temporal_grad = outs
    return (
        section_out[None],
        input_grad[None],
        spatial_grad.reshape(3, 3, 256, 256),
        temporal_grad.reshape(3, 256, 256),
    )


def solution(mesh):
    in_specs = (P("dp", "tm", "height", None, None), P(), P(), P("dp", "tm", "height", None, None))
    out_specs = (P("dp", "tm", "height", None, None), P("dp", "tm", "height", None, None), P(), P())
    return jax.shard_map(
        on_device, mesh=mesh, in_specs=in_specs, out_specs=out_specs, check_vma=False
    )
```

```python
import jax
import jax.numpy as jnp
from jax import lax
from jax.experimental import pallas as pl
from jax.experimental.pallas import tpu as pltpu
from jax.sharding import PartitionSpec as P

F32 = jnp.float32
BF16 = jnp.bfloat16
MESH = pl.DeviceIdType.MESH
CHUNKS = 3
N0, N1, N2, N3 = 64, 8, 2, 1
HALF = N0 // 2
PLACES = (9, 10, 11, 3, 0, 6, 1, 7, 4, 5, 2, 8)
SLOT = [PLACES.index(m) for m in range(12)]
SIZE = dict(x=4, y=4, z=8, c=2)


def place():
    dp, tm, h = lax.axis_index("dp"), lax.axis_index("tm"), lax.axis_index("height")
    return dict(x=tm, y=dp // 2, z=(dp % 2) * 4 + h // 2, c=h % 2)


def device(p):
    return (p["y"] * 2 + p["z"] // 4, p["x"], (p["z"] % 4) * 2 + p["c"])


def peer(me, axis, d):
    return {**me, axis: (me[axis] + d) % SIZE[axis]}


def loop(count, body):
    def step(i, carry):
        body(i)
        return carry

    lax.fori_loop(0, count, step, 0)


def nn(a, b):
    return lax.dot_general(a, b, (((1,), (0,)), ((), ())), preferred_element_type=F32)


def nt(a, b):
    return lax.dot_general(a, b, (((1,), (1,)), ((), ())), preferred_element_type=F32)


SCRATCH = dict(
    wv=pltpu.VMEM((9, 256, 256), BF16),
    tv=pltpu.VMEM((3, 256, 256), BF16),
    low=pltpu.VMEM((6, 6, 32, 256), BF16),
    cot=pltpu.VMEM((6, 8, 64, 256), BF16),
    cotp=pltpu.VMEM((6, 512, 256), BF16),
    tmp=pltpu.VMEM((16, 64, 128), F32),
    ys=pltpu.VMEM((9, 24, 32, 256), F32),
    act=pltpu.VMEM((6, 512, 256), BF16),
    actT=pltpu.VMEM((256, 2048), BF16),
    lowT=pltpu.VMEM((2, 256, 384), BF16),
    tT=pltpu.VMEM((768, 256), BF16),
    ds=pltpu.VMEM((4, 512, 256), F32),
    pg=pltpu.VMEM((4, 10, 64, 256), BF16),
    odd=pltpu.VMEM((3, 4, 7, 32, 256), BF16),
    even=pltpu.VMEM((3, 4, 6, 32, 256), BF16),
    grads=pltpu.VMEM((384, 8, 256), F32),
    ig_acc=pltpu.VMEM((512, 256), F32),
    recv0=pltpu.VMEM((CHUNKS, N0, 8, 256), F32),
    acc=pltpu.VMEM((CHUNKS, N0, 8, 256), F32),
    snd1=pltpu.VMEM((CHUNKS, N0 // 2, 16, 256), BF16),
    recv1=pltpu.VMEM((CHUNKS, 2, 3, N1 // 2, 16, 256), BF16),
    acc1=pltpu.VMEM((CHUNKS, 2, N1, 8, 256), F32),
    recv2=pltpu.VMEM((CHUNKS, 2, 3, N2, 8, 256), F32),
    acc2=pltpu.VMEM((CHUNKS, 2, N2, 8, 256), F32),
    recv3=pltpu.VMEM((CHUNKS, 7, N3, 8, 128), F32),
    mean=pltpu.VMEM((CHUNKS, 2, N2, 8, 256), F32),
    full=pltpu.VMEM((CHUNKS * N0, 16, 256), BF16),
    ssem=pltpu.SemaphoreType.DMA((9 + 40 * CHUNKS,)),
    rsem=pltpu.SemaphoreType.DMA((9 + 40 * CHUNKS,)),
    ready=pltpu.SemaphoreType.REGULAR((5,)),
    lsem=pltpu.SemaphoreType.DMA((24,)),
)


def kernel(low_hbm, w_hbm, t_hbm, cot_hbm, so_v, ig_v, s_v, tg_v, *scratch):
    s = dict(zip(SCRATCH, scratch))
    low, cot, cotp, ys, act, ds, pg = (s[n] for n in ("low", "cot", "cotp", "ys", "act", "ds", "pg"))
    odd, even, grads, tmp, full = (s[n] for n in ("odd", "even", "grads", "tmp", "full"))
    wv, tv = s["wv"], s["tv"]
    me = place()
    dp, tm, h = lax.axis_index("dp"), lax.axis_index("tm"), lax.axis_index("height")
    yes = True
    barrier = pltpu.get_barrier_semaphore()
    near = [device(peer(me, axis, d)) for axis in "xyz" for d in (1, SIZE[axis] - 1)]
    others = [device(peer(me, "c", 1))] + near
    others += [(dp, (tm + i) % 4, (h + j) % 8) for i in (0, 1, 3) for j in (1, 7)]
    for to in others:
        pl.semaphore_signal(barrier, inc=1, device_id=to, device_id_type=MESH)

    local_used = [0]

    def local(src, dst):
        copy = pltpu.make_async_copy(src, dst, s["lsem"].at[local_used[0]])
        local_used[0] += 1
        copy.start()
        return copy

    load_low = local(low_hbm, low.at[pl.ds(2, 4), pl.ds(1, 4)])
    load_w = local(w_hbm, wv)
    load_cot = local(cot_hbm, cot.at[pl.ds(0, 4)])
    load_t = local(t_hbm, tv)

    @pl.when(tm == 0)
    def _():
        low[0:2] = jnp.zeros((2, 6, 32, 256), BF16)

    @pl.when(tm == 3)
    def _():
        cot[4:6] = jnp.zeros((2, 8, 64, 256), BF16)

    @pl.when(h == 0)
    def _():
        low[2:6, 0] = jnp.zeros((4, 32, 256), BF16)
        pg[:, 0] = jnp.zeros((4, 64, 256), BF16)

    @pl.when(h == 7)
    def _():
        low[2:6, 5] = jnp.zeros((4, 32, 256), BF16)
        pg[:, 9] = jnp.zeros((4, 64, 256), BF16)

    @pl.when((h == 0) & (tm > 0))
    def _():
        low[0:2, 0] = jnp.zeros((2, 32, 256), BF16)

    @pl.when((h == 7) & (tm > 0))
    def _():
        low[0:2, 5] = jnp.zeros((2, 32, 256), BF16)

    pl.semaphore_wait(barrier, len(others))
    used = [0]
    halos = []

    def halo(src, dst, to, sends, receives):
        k = used[0]
        used[0] += 1
        copy = pltpu.make_async_remote_copy(
            src_ref=src, dst_ref=dst, send_sem=s["ssem"].at[k], recv_sem=s["rsem"].at[k],
            device_id=to, device_id_type=MESH,
        )

        @pl.when(sends)
        def _():
            copy.start()

        halos.append((copy, sends))
        return copy, receives

    def arrive(pair):
        copy, receives = pair

        @pl.when(receives)
        def _():
            copy.wait_recv()

    up, down, right, left = (h + 1) % 8, (h + 7) % 8, (tm + 1) % 4, (tm + 3) % 4
    own, early = pl.ds(2, 4), pl.ds(0, 2)
    low_up = halo(low_hbm.at[:, 3], low.at[own, 0], (dp, tm, up), h < 7, h > 0)
    low_down = halo(low_hbm.at[:, 0], low.at[own, 5], (dp, tm, down), h > 0, h < 7)
    cots = [
        halo(cot_hbm.at[f], cot.at[4 + f], (dp, left, h), tm > 0, tm < 3) for f in range(2)
    ]
    last = pl.ds(2, 2)
    early_low = [
        halo(low_hbm.at[last], low.at[early, pl.ds(1, 4)], (dp, right, h), tm < 3, tm > 0),
        halo(low_hbm.at[last, 3], low.at[early, 0], (dp, right, up), (tm < 3) & (h < 7), (tm > 0) & (h > 0)),
        halo(low_hbm.at[last, 0], low.at[early, 5], (dp, right, down), (tm < 3) & (h > 0), (tm > 0) & (h < 7)),
    ]

    def tell(slot, axis):
        for d in (1, SIZE[axis] - 1):
            to = device(peer(me, axis, d))
            pl.semaphore_signal(s["ready"].at[slot], inc=1, device_id=to, device_id_type=MESH)

    for slot, axis in enumerate("xyz"):
        tell(slot, axis)

    def split_columns(f):
        for y in range(8):
            for half in range(2):
                tmp[y * 2 + half] = cot[f, y, :, half * 128 : half * 128 + 128].astype(F32)
        for y in range(8):
            for half in range(2):
                for b in range(2):
                    part = tmp[y * 2 + half, pl.ds(b, 32, stride=2), :]
                    at = pl.ds(y * 64 + b * 32, 32)
                    cotp[f, at, half * 128 : half * 128 + 128] = part.astype(BF16)

    load_cot.wait()
    loop(4, split_columns)
    load_low.wait()
    load_w.wait()
    load_t.wait()
    for k in range(3):
        s["tT"][256 * k : 256 * k + 256] = tv[k].T
    arrive(low_up)
    arrive(low_down)
    col = lax.broadcasted_iota(jnp.int32, (32, 256), 0)

    def from_left(v):
        return jnp.where(col == 0, 0.0, pltpu.roll(v, 1, 0))

    def from_right(v):
        return jnp.where(col == 31, 0.0, pltpu.roll(v, 31, 0))

    def products(first, count):
        def one(ij):
            rows = low[pl.ds(first, count)].reshape(count * 192, 256)
            ys[ij, 0 : count * 6] = nn(rows, wv[ij]).reshape(count * 6, 32, 256)

        loop(9, one)

    def activate(first, count, slopes):
        def one(n):
            f, r = n // 4, n % 4
            at = f * 6 + r + 1
            for a in range(2):
                z = [ys[j, at - 1 + a] + ys[3 + j, at] + ys[6 + j, at + a] for j in range(3)]
                pres = (from_left(z[0]) + z[1] + z[2], z[0] + z[1] + from_right(z[2]))
                for b in range(2):
                    pre = pres[b]
                    sig = 0.5 * jnp.tanh(0.5 * pre) + 0.5
                    tokens = pl.ds((r * 2 + a) * 64 + b * 32, 32)
                    act[first + f, tokens] = (pre * sig).astype(BF16)
                    if slopes:
                        ds[f, tokens] = sig * (1.0 + pre * (1.0 - sig))

        loop(count * 4, one)

    products(2, 4)
    for slot in range(3):
        pl.semaphore_wait(s["ready"].at[slot], 2)
    tell(3, "z")
    activate(2, 4, True)
    pl.semaphore_wait(s["ready"].at[3], 2)
    tell(4, "z")

    for f in range(4):
        s["actT"][:, 512 * f : 512 * f + 512] = act[2 + f].T
    for half in range(2):
        s["lowT"][half] = low[2 + 2 * half : 4 + 2 * half].reshape(384, 256).T
    pad = jnp.zeros((3, 4, 32, 256), BF16)
    odd[:, :, 0] = pad
    odd[:, :, 6] = pad
    even[:, :, 0] = pad
    even[:, :, 5] = pad

    def pre_grad(f):
        total = nn(jnp.concatenate([cotp[f + k] for k in range(3)], 1), s["tT"][...])
        pg[f, 1:9] = (total * ds[f]).astype(BF16).reshape(8, 64, 256)

    def put(ref, f, q, even_cols, odd_cols):
        ref[0, f, q + 1] = (odd_cols + from_right(even_cols)).astype(BF16)
        ref[1, f, q + 1] = (odd_cols + even_cols).astype(BF16)
        ref[2, f, q + 1] = (from_left(odd_cols) + even_cols).astype(BF16)

    def rows_of(f, slots):
        halves = []
        for b in range(2):
            total = pg[f, slots[0], b * 32 : b * 32 + 32].astype(F32)
            for slot in slots[1:]:
                total = total + pg[f, slot, b * 32 : b * 32 + 32].astype(F32)
            halves.append(total)
        return halves

    def box(f):
        for q in range(5):
            slots = [n for n in (2 * q, 2 * q + 1) if 0 < n < 9]
            put(odd, f, q, *rows_of(f, slots))
        for r in range(4):
            put(even, f, r, *rows_of(f, (2 * r + 1, 2 * r + 2)))

    def weight_grad(m, half):
        i, j = m // 3, m % 3
        two = pl.ds(2 * half, 2)
        sums = (odd[j, two, 1:7], even[j, two], odd[j, two, 0:6])[i]
        total = nn(s["lowT"][half], sums.reshape(384, 256))
        add_to(m, total, half == 0)

    def add_to(m, total, fresh):
        at = pl.ds(SLOT[m] * 32, 32)
        total = total.reshape(32, 8, 256)
        grads[at] = total if fresh else grads[at] + total

    def temporal(k, frames, fresh):
        a, b = frames[0], frames[-1] + 1
        grad = cotp[a + k : b + k].reshape((b - a) * 512, 256)
        total = nn(s["actT"][:, 512 * a : 512 * b], grad)
        add_to(9 + k, total, fresh)

    loop(2, pre_grad)
    pl.semaphore_wait(s["ready"].at[4], 2)
    loop(2, box)
    for k in range(3):
        temporal(k, range(4 - k), True)
    for m in range(9):
        weight_grad(m, 0)
    arrive(cots[0])
    split_columns(4)
    pre_grad(2)
    temporal(1, (3,), False)
    temporal(2, (2,), False)
    box(2)
    arrive(cots[1])
    split_columns(5)
    pre_grad(3)
    pg_up = halo(pg.at[:, 8], pg.at[:, 0], (dp, tm, up), h < 7, h > 0)
    pg_down = halo(pg.at[:, 1], pg.at[:, 9], (dp, tm, down), h > 0, h < 7)
    temporal(2, (3,), False)
    box(3)

    def early():
        for pair in early_low:
            arrive(pair)
        products(0, 2)
        activate(0, 2, False)

    def section(t):
        total = nn(jnp.concatenate([act[t + 2 - k] for k in range(3)], 1), tv[...].reshape(768, 256))
        for y in range(8):
            up_row = low[t + 2, y // 2 + 1].astype(F32)
            for b in range(2):
                at = y * 64 + b * 32
                value = total[at : at + 32] + up_row
                for half in range(2):
                    tmp[y * 2 + half, pl.ds(b, 32, stride=2), :] = value[:, half * 128 : half * 128 + 128]
        for y in range(8):
            for half in range(2):
                so_v[t, y, :, half * 128 : half * 128 + 128] = tmp[y * 2 + half].astype(BF16)

    started = []

    def send(src, dst, to):
        k = used[0]
        used[0] += 1
        copy = pltpu.make_async_remote_copy(
            src_ref=src, dst_ref=dst, send_sem=s["ssem"].at[k], recv_sem=s["rsem"].at[k],
            device_id=device(to), device_id_type=MESH,
        )
        copy.start()
        started.append(copy)
        return copy

    c, z = me["c"], me["z"]
    order = (("x", "y"), ("y", "x"))
    recv0, acc, snd1, recv1, acc1, recv2, acc2, recv3 = (
        s[n] for n in ("recv0", "acc", "snd1", "recv1", "acc1", "recv2", "acc2", "recv3")
    )

    def base(k):
        return k * 2 * N0 + c * N0

    def zslice(to):
        return pl.ds((to % 4) // 2, N3), slice(None), pl.ds(pl.multiple_of((to % 2) * 128, 128), 128)

    def stage0(k):
        for m in PLACES[4 * k : 4 * k + 4]:
            if m < 9:
                weight_grad(m, 1)
        return [send(grads.at[pl.ds(k * 2 * N0 + (1 - c) * N0, N0)], recv0.at[k], peer(me, "c", 1))]

    def stage1(k):
        def add(i):
            at = pl.ds(i * 8, 8)
            total = grads[pl.ds(base(k) + i * 8, 8)] + recv0[k, at]
            acc[k, at] = total
            snd1[k, pl.ds(i * 4, 4)] = total.reshape(4, 16, 256).astype(BF16)

        loop(N0 // 8, add)
        copies = []
        for part in range(2):
            axis = order[part][0]
            for d in range(1, 4):
                to = peer(me, axis, d)
                src = snd1.at[k, pl.ds((part * HALF + to[axis] * N1) // 2, N1 // 2)]
                copies.append(send(src, recv1.at[k, part, d - 1], to))
        return copies

    def stage2(k):
        for part in range(2):
            total = acc[k, pl.ds(part * HALF + me[order[part][0]] * N1, N1)]
            for d in range(3):
                total = total + recv1[k, part, d].astype(F32).reshape(N1, 8, 256)
            acc1[k, part] = total
        copies = []
        for part in range(2):
            axis = order[part][1]
            for d in range(1, 4):
                to = peer(me, axis, d)
                copies.append(send(acc1.at[k, part, pl.ds(to[axis] * N2, N2)], recv2.at[k, part, d - 1], to))
        return copies

    def stage3(k):
        for part in range(2):
            total = acc1[k, part, pl.ds(me[order[part][1]] * N2, N2)]
            for d in range(3):
                total = total + recv2[k, part, d]
            acc2[k, part] = total
        copies = []
        for d in range(1, 8):
            to = peer(me, "z", d)
            copies.append(send(acc2.at[(k, to["z"] // 4, *zslice(to["z"]))], recv3.at[k, d - 1], to))
        return copies

    def stage4(k):
        total = acc2[(k, z // 4, *zslice(z))]
        for d in range(7):
            total = total + recv3[k, d]
        shard = s["mean"].at[(k, z // 4, *zslice(z))]
        shard[...] = total
        return [send(shard, shard, peer(me, "z", d)) for d in range(1, 8)]

    def unit(k, n):
        return k * N0 + (c * N0 + n) // 2

    def spread_by(k, depth):
        copies = []
        for part in range(2):
            a, b = order[part]
            if depth == 2:
                n = unit(k, part * HALF + me[a] * N1 + me[b] * N2)
                full[n] = s["mean"][k, part].reshape(16, 256).astype(BF16)
                at, axis = pl.ds(n, N2 // 2), b
            else:
                at, axis = pl.ds(unit(k, part * HALF + me[a] * N1), N1 // 2), a
            copies += [send(full.at[at], full.at[at], peer(me, axis, d)) for d in range(1, 4)]
        return copies

    def stage5(k):
        return spread_by(k, 2)

    def stage6(k):
        return spread_by(k, 1)

    def stage7(k):
        at = pl.ds(unit(k, 0), N0 // 2)
        return [send(full.at[at], full.at[at], peer(me, "c", 1))]

    def stage8(k):
        for n in range(4 * k, 4 * k + 4):
            m = PLACES[n]
            ref, at = (s_v, m) if m < 9 else (tg_v, m - 9)

            def widen(i, n=n, ref=ref, at=at):
                ref[pl.ds(at * 32 + i * 8, 8)] = full[pl.ds(n * 16 + i * 4, 4)].astype(F32).reshape(8, 8, 256)

            loop(4, widen)
        return []

    def edge(f):
        put(odd, f, 0, *rows_of(f, (0, 1)))
        put(odd, f, 4, *rows_of(f, (8, 9)))

    def cot_sum(n):
        f, r = n // 4, n % 4
        total = jnp.zeros((32, 256), F32)
        for q in range(4):
            total = total + cotp[f, pl.ds(r * 128 + q * 32, 32)].astype(F32)
        s["ig_acc"][pl.ds(n * 32, 32)] = total

    def inputs(j):
        total = nt(odd[j, :, 2:6].reshape(512, 256), wv[j])
        total = total + nt(even[j, :, 1:5].reshape(512, 256), wv[3 + j])
        total = total + nt(odd[j, :, 1:5].reshape(512, 256), wv[6 + j])
        s["ig_acc"][...] += total

    def input_grad():
        arrive(pg_up)
        arrive(pg_down)
        loop(4, edge)
        loop(16, cot_sum)
        loop(3, inputs)
        ig_v[...] = s["ig_acc"][...].astype(BF16).reshape(4, 4, 32, 256)

    stages = (stage0, stage1, stage2, stage3, stage4, stage5, stage6, stage7, stage8)
    flying = [[] for _ in range(CHUNKS)]
    for stage in stages:
        for k in range(CHUNKS):
            for copy in flying[k]:
                copy.wait_recv()
            flying[k] = stage(k)
        if stage is stage1:
            input_grad()
        if stage is stage2:
            early()
        if stage is stage3:
            loop(2, section)
        if stage is stage4:
            loop(2, lambda t: section(t + 2))
    for copy in started:
        copy.wait_send()
    for copy, sends in halos:

        @pl.when(sends)
        def _(copy=copy):
            copy.wait_send()


def store(so_v, ig_v, s_v, tg_v, so, ig, sg, tg, sems):
    copies = [
        pltpu.make_async_copy(src, dst, sems.at[n])
        for n, (src, dst) in enumerate(((so_v, so), (s_v, sg), (tg_v, tg), (ig_v, ig)))
    ]
    for copy in copies:
        copy.start()
    for copy in copies:
        copy.wait()


def on_device(low_frames, spatial_weight, temporal_weight, cotangent):
    hbm = pl.BlockSpec(memory_space=pltpu.HBM)
    vmem = pl.BlockSpec(memory_space=pltpu.VMEM)
    shapes = (
        jax.ShapeDtypeStruct((4, 8, 64, 256), BF16),
        jax.ShapeDtypeStruct((4, 4, 32, 256), BF16),
        jax.ShapeDtypeStruct((288, 8, 256), F32),
        jax.ShapeDtypeStruct((96, 8, 256), F32),
    )
    held = pl.pallas_call(
        kernel,
        out_shape=tuple(pltpu.VMEM(a.shape, a.dtype) for a in shapes),
        in_specs=[hbm] * 4,
        out_specs=(vmem,) * 4,
        scratch_shapes=list(SCRATCH.values()),
        compiler_params=pltpu.CompilerParams(
            collective_id=0, has_side_effects=True, vmem_limit_bytes=52 << 20
        ),
        name="section",
    )(low_frames[0], spatial_weight.reshape(9, 256, 256), temporal_weight, cotangent[0])
    outs = pl.pallas_call(
        store,
        out_shape=shapes,
        in_specs=[vmem] * 4,
        out_specs=(hbm,) * 4,
        scratch_shapes=[pltpu.SemaphoreType.DMA((4,))],
        compiler_params=pltpu.CompilerParams(vmem_limit_bytes=4 << 20),
        name="store",
    )(*(pltpu.with_memory_space_constraint(a, pltpu.VMEM) for a in held))
    section_out, input_grad, spatial_grad, temporal_grad = outs
    return (
        section_out[None],
        input_grad[None],
        spatial_grad.reshape(3, 3, 256, 256),
        temporal_grad.reshape(3, 256, 256),
    )


def solution(mesh):
    in_specs = (P("dp", "tm", "height", None, None), P(), P(), P("dp", "tm", "height", None, None))
    out_specs = (P("dp", "tm", "height", None, None), P("dp", "tm", "height", None, None), P(), P())
    return jax.shard_map(
        on_device, mesh=mesh, in_specs=in_specs, out_specs=out_specs, check_vma=False
    )
```

```python
import jax
import jax.numpy as jnp
from jax import lax
from jax.experimental import pallas as pl
from jax.experimental.pallas import tpu as pltpu
from jax.sharding import PartitionSpec as P

F32 = jnp.float32
BF16 = jnp.bfloat16
MESH = pl.DeviceIdType.MESH
CHUNKS = 3
N0, N1, N2, N3 = 64, 8, 2, 1
HALF = N0 // 2
FAR_FIRST = (4, 3, 5, 2, 6, 1, 7)
PLACES = (9, 10, 11, 3, 0, 6, 1, 7, 4, 5, 2, 8)
SLOT = [PLACES.index(m) for m in range(12)]
SIZE = dict(x=4, y=4, z=8, c=2)


def place():
    dp, tm, h = lax.axis_index("dp"), lax.axis_index("tm"), lax.axis_index("height")
    return dict(x=tm, y=dp // 2, z=(dp % 2) * 4 + h // 2, c=h % 2)


def device(p):
    return (p["y"] * 2 + p["z"] // 4, p["x"], (p["z"] % 4) * 2 + p["c"])


def peer(me, axis, d):
    return {**me, axis: (me[axis] + d) % SIZE[axis]}


def loop(count, body):
    def step(i, carry):
        body(i)
        return carry

    lax.fori_loop(0, count, step, 0)


def nn(a, b):
    return lax.dot_general(a, b, (((1,), (0,)), ((), ())), preferred_element_type=F32)


def nt(a, b):
    return lax.dot_general(a, b, (((1,), (1,)), ((), ())), preferred_element_type=F32)


SCRATCH = dict(
    wv=pltpu.VMEM((9, 256, 256), BF16),
    tv=pltpu.VMEM((3, 256, 256), BF16),
    low=pltpu.VMEM((6, 6, 32, 256), BF16),
    cot=pltpu.VMEM((6, 8, 64, 256), BF16),
    cotp=pltpu.VMEM((6, 512, 256), BF16),
    tmp=pltpu.VMEM((16, 64, 128), F32),
    ys=pltpu.VMEM((9, 24, 32, 256), F32),
    act=pltpu.VMEM((6, 512, 256), BF16),
    actT=pltpu.VMEM((256, 2048), BF16),
    lowT=pltpu.VMEM((2, 256, 384), BF16),
    tT=pltpu.VMEM((768, 256), BF16),
    ds=pltpu.VMEM((4, 512, 256), F32),
    pg=pltpu.VMEM((4, 10, 64, 256), BF16),
    odd=pltpu.VMEM((3, 4, 7, 32, 256), BF16),
    even=pltpu.VMEM((3, 4, 6, 32, 256), BF16),
    grads=pltpu.VMEM((384, 8, 256), F32),
    ig_acc=pltpu.VMEM((512, 256), F32),
    recv0=pltpu.VMEM((CHUNKS, N0, 8, 256), F32),
    acc=pltpu.VMEM((CHUNKS, N0, 8, 256), F32),
    snd1=pltpu.VMEM((CHUNKS, N0 // 2, 16, 256), BF16),
    recv1=pltpu.VMEM((CHUNKS, 2, 3, N1 // 2, 16, 256), BF16),
    acc1=pltpu.VMEM((CHUNKS, 2, N1, 8, 256), F32),
    recv2=pltpu.VMEM((CHUNKS, 2, 3, N2, 8, 256), F32),
    acc2=pltpu.VMEM((CHUNKS, 2, N2, 8, 256), F32),
    recv3=pltpu.VMEM((CHUNKS, 7, N3, 8, 128), F32),
    mean=pltpu.VMEM((CHUNKS, 2, N2, 8, 256), F32),
    full=pltpu.VMEM((CHUNKS * N0, 16, 256), BF16),
    ssem=pltpu.SemaphoreType.DMA((9 + 40 * CHUNKS,)),
    rsem=pltpu.SemaphoreType.DMA((9 + 40 * CHUNKS,)),
    ready=pltpu.SemaphoreType.REGULAR((5,)),
    lsem=pltpu.SemaphoreType.DMA((24,)),
)


def kernel(low_hbm, w_hbm, t_hbm, cot_hbm, so_v, ig_v, s_v, tg_v, *scratch):
    s = dict(zip(SCRATCH, scratch))
    low, cot, cotp, ys, act, ds, pg = (s[n] for n in ("low", "cot", "cotp", "ys", "act", "ds", "pg"))
    odd, even, grads, tmp, full = (s[n] for n in ("odd", "even", "grads", "tmp", "full"))
    wv, tv = s["wv"], s["tv"]
    me = place()
    dp, tm, h = lax.axis_index("dp"), lax.axis_index("tm"), lax.axis_index("height")
    yes = True
    barrier = pltpu.get_barrier_semaphore()
    near = [device(peer(me, axis, d)) for axis in "xyz" for d in (1, SIZE[axis] - 1)]
    others = [device(peer(me, "c", 1))] + near
    others += [(dp, (tm + i) % 4, (h + j) % 8) for i in (0, 1, 3) for j in (1, 7)]
    for to in others:
        pl.semaphore_signal(barrier, inc=1, device_id=to, device_id_type=MESH)

    local_used = [0]

    def local(src, dst):
        copy = pltpu.make_async_copy(src, dst, s["lsem"].at[local_used[0]])
        local_used[0] += 1
        copy.start()
        return copy

    load_low = local(low_hbm, low.at[pl.ds(2, 4), pl.ds(1, 4)])
    load_w = local(w_hbm, wv)
    load_cot = local(cot_hbm, cot.at[pl.ds(0, 4)])
    load_t = local(t_hbm, tv)

    @pl.when(tm == 0)
    def _():
        low[0:2] = jnp.zeros((2, 6, 32, 256), BF16)

    @pl.when(tm == 3)
    def _():
        cot[4:6] = jnp.zeros((2, 8, 64, 256), BF16)

    @pl.when(h == 0)
    def _():
        low[2:6, 0] = jnp.zeros((4, 32, 256), BF16)
        pg[:, 0] = jnp.zeros((4, 64, 256), BF16)

    @pl.when(h == 7)
    def _():
        low[2:6, 5] = jnp.zeros((4, 32, 256), BF16)
        pg[:, 9] = jnp.zeros((4, 64, 256), BF16)

    @pl.when((h == 0) & (tm > 0))
    def _():
        low[0:2, 0] = jnp.zeros((2, 32, 256), BF16)

    @pl.when((h == 7) & (tm > 0))
    def _():
        low[0:2, 5] = jnp.zeros((2, 32, 256), BF16)

    pl.semaphore_wait(barrier, len(others))
    used = [0]
    halos = []

    def halo(src, dst, to, sends, receives):
        k = used[0]
        used[0] += 1
        copy = pltpu.make_async_remote_copy(
            src_ref=src, dst_ref=dst, send_sem=s["ssem"].at[k], recv_sem=s["rsem"].at[k],
            device_id=to, device_id_type=MESH,
        )

        @pl.when(sends)
        def _():
            copy.start()

        halos.append((copy, sends))
        return copy, receives

    def arrive(pair):
        copy, receives = pair

        @pl.when(receives)
        def _():
            copy.wait_recv()

    up, down, right, left = (h + 1) % 8, (h + 7) % 8, (tm + 1) % 4, (tm + 3) % 4
    own, early = pl.ds(2, 4), pl.ds(0, 2)
    low_up = halo(low_hbm.at[:, 3], low.at[own, 0], (dp, tm, up), h < 7, h > 0)
    low_down = halo(low_hbm.at[:, 0], low.at[own, 5], (dp, tm, down), h > 0, h < 7)
    cots = [
        halo(cot_hbm.at[f], cot.at[4 + f], (dp, left, h), tm > 0, tm < 3) for f in range(2)
    ]
    last = pl.ds(2, 2)
    early_low = [
        halo(low_hbm.at[last], low.at[early, pl.ds(1, 4)], (dp, right, h), tm < 3, tm > 0),
        halo(low_hbm.at[last, 3], low.at[early, 0], (dp, right, up), (tm < 3) & (h < 7), (tm > 0) & (h > 0)),
        halo(low_hbm.at[last, 0], low.at[early, 5], (dp, right, down), (tm < 3) & (h > 0), (tm > 0) & (h < 7)),
    ]

    def tell(slot, axis):
        for d in (1, SIZE[axis] - 1):
            to = device(peer(me, axis, d))
            pl.semaphore_signal(s["ready"].at[slot], inc=1, device_id=to, device_id_type=MESH)

    for slot, axis in enumerate("xyz"):
        tell(slot, axis)

    def split_columns(f):
        for y in range(8):
            for half in range(2):
                tmp[y * 2 + half] = cot[f, y, :, half * 128 : half * 128 + 128].astype(F32)
        for y in range(8):
            for half in range(2):
                for b in range(2):
                    part = tmp[y * 2 + half, pl.ds(b, 32, stride=2), :]
                    at = pl.ds(y * 64 + b * 32, 32)
                    cotp[f, at, half * 128 : half * 128 + 128] = part.astype(BF16)

    load_cot.wait()
    loop(4, split_columns)
    load_low.wait()
    load_w.wait()
    load_t.wait()
    for k in range(3):
        s["tT"][256 * k : 256 * k + 256] = tv[k].T
    arrive(low_up)
    arrive(low_down)
    col = lax.broadcasted_iota(jnp.int32, (32, 256), 0)

    def from_left(v):
        return jnp.where(col == 0, 0.0, pltpu.roll(v, 1, 0))

    def from_right(v):
        return jnp.where(col == 31, 0.0, pltpu.roll(v, 31, 0))

    def products(first, count):
        def one(ij):
            rows = low[pl.ds(first, count)].reshape(count * 192, 256)
            ys[ij, 0 : count * 6] = nn(rows, wv[ij]).reshape(count * 6, 32, 256)

        loop(9, one)

    def activate(first, count, slopes):
        def one(n):
            f, r = n // 4, n % 4
            at = f * 6 + r + 1
            for a in range(2):
                z = [ys[j, at - 1 + a] + ys[3 + j, at] + ys[6 + j, at + a] for j in range(3)]
                pres = (from_left(z[0]) + z[1] + z[2], z[0] + z[1] + from_right(z[2]))
                for b in range(2):
                    pre = pres[b]
                    sig = 0.5 * jnp.tanh(0.5 * pre) + 0.5
                    tokens = pl.ds((r * 2 + a) * 64 + b * 32, 32)
                    act[first + f, tokens] = (pre * sig).astype(BF16)
                    if slopes:
                        ds[f, tokens] = sig * (1.0 + pre * (1.0 - sig))

        loop(count * 4, one)

    products(2, 4)
    for slot in range(3):
        pl.semaphore_wait(s["ready"].at[slot], 2)
    tell(3, "z")
    activate(2, 4, True)
    pl.semaphore_wait(s["ready"].at[3], 2)
    tell(4, "z")

    for f in range(4):
        s["actT"][:, 512 * f : 512 * f + 512] = act[2 + f].T
    for half in range(2):
        s["lowT"][half] = low[2 + 2 * half : 4 + 2 * half].reshape(384, 256).T
    pad = jnp.zeros((3, 4, 32, 256), BF16)
    odd[:, :, 0] = pad
    odd[:, :, 6] = pad
    even[:, :, 0] = pad
    even[:, :, 5] = pad

    def pre_grad(f):
        total = nn(jnp.concatenate([cotp[f + k] for k in range(3)], 1), s["tT"][...])
        pg[f, 1:9] = (total * ds[f]).astype(BF16).reshape(8, 64, 256)

    def put(ref, f, q, even_cols, odd_cols):
        ref[0, f, q + 1] = (odd_cols + from_right(even_cols)).astype(BF16)
        ref[1, f, q + 1] = (odd_cols + even_cols).astype(BF16)
        ref[2, f, q + 1] = (from_left(odd_cols) + even_cols).astype(BF16)

    def rows_of(f, slots):
        halves = []
        for b in range(2):
            total = pg[f, slots[0], b * 32 : b * 32 + 32].astype(F32)
            for slot in slots[1:]:
                total = total + pg[f, slot, b * 32 : b * 32 + 32].astype(F32)
            halves.append(total)
        return halves

    def box(f):
        for q in range(5):
            slots = [n for n in (2 * q, 2 * q + 1) if 0 < n < 9]
            put(odd, f, q, *rows_of(f, slots))
        for r in range(4):
            put(even, f, r, *rows_of(f, (2 * r + 1, 2 * r + 2)))

    def weight_grad(m, half):
        i, j = m // 3, m % 3
        two = pl.ds(2 * half, 2)
        sums = (odd[j, two, 1:7], even[j, two], odd[j, two, 0:6])[i]
        total = nn(s["lowT"][half], sums.reshape(384, 256))
        add_to(m, total, half == 0)

    def add_to(m, total, fresh):
        at = pl.ds(SLOT[m] * 32, 32)
        total = total.reshape(32, 8, 256)
        grads[at] = total if fresh else grads[at] + total

    def temporal(k, frames, fresh):
        a, b = frames[0], frames[-1] + 1
        grad = cotp[a + k : b + k].reshape((b - a) * 512, 256)
        total = nn(s["actT"][:, 512 * a : 512 * b], grad)
        add_to(9 + k, total, fresh)

    loop(2, pre_grad)
    pl.semaphore_wait(s["ready"].at[4], 2)
    loop(2, box)
    for k in range(3):
        temporal(k, range(4 - k), True)
    for m in range(9):
        weight_grad(m, 0)
    arrive(cots[0])
    split_columns(4)
    pre_grad(2)
    temporal(1, (3,), False)
    temporal(2, (2,), False)
    box(2)
    arrive(cots[1])
    split_columns(5)
    pre_grad(3)
    pg_up = halo(pg.at[:, 8], pg.at[:, 0], (dp, tm, up), h < 7, h > 0)
    pg_down = halo(pg.at[:, 1], pg.at[:, 9], (dp, tm, down), h > 0, h < 7)
    temporal(2, (3,), False)
    box(3)

    def early():
        for pair in early_low:
            arrive(pair)
        products(0, 2)
        activate(0, 2, False)

    def section(t):
        total = nn(jnp.concatenate([act[t + 2 - k] for k in range(3)], 1), tv[...].reshape(768, 256))
        for y in range(8):
            up_row = low[t + 2, y // 2 + 1].astype(F32)
            for b in range(2):
                at = y * 64 + b * 32
                value = total[at : at + 32] + up_row
                for half in range(2):
                    tmp[y * 2 + half, pl.ds(b, 32, stride=2), :] = value[:, half * 128 : half * 128 + 128]
        for y in range(8):
            for half in range(2):
                so_v[t, y, :, half * 128 : half * 128 + 128] = tmp[y * 2 + half].astype(BF16)

    def send(src, dst, to):
        k = used[0]
        used[0] += 1
        copy = pltpu.make_async_remote_copy(
            src_ref=src, dst_ref=dst, send_sem=s["ssem"].at[k], recv_sem=s["rsem"].at[k],
            device_id=device(to), device_id_type=MESH,
        )
        copy.start()
        return copy

    c, z = me["c"], me["z"]
    order = (("x", "y"), ("y", "x"))
    recv0, acc, snd1, recv1, acc1, recv2, acc2, recv3 = (
        s[n] for n in ("recv0", "acc", "snd1", "recv1", "acc1", "recv2", "acc2", "recv3")
    )

    def base(k):
        return k * 2 * N0 + c * N0

    def zslice(to):
        return pl.ds((to % 4) // 2, N3), slice(None), pl.ds(pl.multiple_of((to % 2) * 128, 128), 128)

    def stage0(k):
        for m in PLACES[4 * k : 4 * k + 4]:
            if m < 9:
                weight_grad(m, 1)
        return [send(grads.at[pl.ds(k * 2 * N0 + (1 - c) * N0, N0)], recv0.at[k], peer(me, "c", 1))]

    def stage1(k):
        def add(i):
            at = pl.ds(i * 8, 8)
            total = grads[pl.ds(base(k) + i * 8, 8)] + recv0[k, at]
            acc[k, at] = total
            snd1[k, pl.ds(i * 4, 4)] = total.reshape(4, 16, 256).astype(BF16)

        loop(N0 // 8, add)
        copies = []
        for part in range(2):
            axis = order[part][0]
            for d in (2, 1, 3):
                to = peer(me, axis, d)
                src = snd1.at[k, pl.ds((part * HALF + to[axis] * N1) // 2, N1 // 2)]
                copies.append(send(src, recv1.at[k, part, d - 1], to))
        return copies

    def stage2(k):
        for part in range(2):
            total = acc[k, pl.ds(part * HALF + me[order[part][0]] * N1, N1)]
            for d in range(3):
                total = total + recv1[k, part, d].astype(F32).reshape(N1, 8, 256)
            acc1[k, part] = total
        copies = []
        for part in range(2):
            axis = order[part][1]
            for d in (2, 1, 3):
                to = peer(me, axis, d)
                copies.append(send(acc1.at[k, part, pl.ds(to[axis] * N2, N2)], recv2.at[k, part, d - 1], to))
        return copies

    def stage3(k):
        for part in range(2):
            total = acc1[k, part, pl.ds(me[order[part][1]] * N2, N2)]
            for d in range(3):
                total = total + recv2[k, part, d]
            acc2[k, part] = total
        copies = []
        for d in FAR_FIRST:
            to = peer(me, "z", d)
            copies.append(send(acc2.at[(k, to["z"] // 4, *zslice(to["z"]))], recv3.at[k, d - 1], to))
        return copies

    def stage4(k):
        total = acc2[(k, z // 4, *zslice(z))]
        for d in range(7):
            total = total + recv3[k, d]
        shard = s["mean"].at[(k, z // 4, *zslice(z))]
        shard[...] = total
        return [send(shard, shard, peer(me, "z", d)) for d in FAR_FIRST]

    def unit(k, n):
        return k * N0 + (c * N0 + n) // 2

    def spread_by(k, depth):
        copies = []
        for part in range(2):
            a, b = order[part]
            if depth == 2:
                n = unit(k, part * HALF + me[a] * N1 + me[b] * N2)
                full[n] = s["mean"][k, part].reshape(16, 256).astype(BF16)
                at, axis = pl.ds(n, N2 // 2), b
            else:
                at, axis = pl.ds(unit(k, part * HALF + me[a] * N1), N1 // 2), a
            copies += [send(full.at[at], full.at[at], peer(me, axis, d)) for d in (2, 1, 3)]
        return copies

    def stage5(k):
        return spread_by(k, 2)

    def stage6(k):
        return spread_by(k, 1)

    def stage7(k):
        at = pl.ds(unit(k, 0), N0 // 2)
        return [send(full.at[at], full.at[at], peer(me, "c", 1))]

    def stage8(k):
        for n in range(4 * k, 4 * k + 4):
            m = PLACES[n]
            ref, at = (s_v, m) if m < 9 else (tg_v, m - 9)

            def widen(i, n=n, ref=ref, at=at):
                ref[pl.ds(at * 32 + i * 8, 8)] = full[pl.ds(n * 16 + i * 4, 4)].astype(F32).reshape(8, 8, 256)

            loop(4, widen)
        return []

    def edge(f):
        put(odd, f, 0, *rows_of(f, (0, 1)))
        put(odd, f, 4, *rows_of(f, (8, 9)))

    def cot_sum(n):
        f, r = n // 4, n % 4
        total = jnp.zeros((32, 256), F32)
        for q in range(4):
            total = total + cotp[f, pl.ds(r * 128 + q * 32, 32)].astype(F32)
        s["ig_acc"][pl.ds(n * 32, 32)] = total

    def inputs(j):
        total = nt(odd[j, :, 2:6].reshape(512, 256), wv[j])
        total = total + nt(even[j, :, 1:5].reshape(512, 256), wv[3 + j])
        total = total + nt(odd[j, :, 1:5].reshape(512, 256), wv[6 + j])
        s["ig_acc"][...] += total

    def input_grad():
        arrive(pg_up)
        arrive(pg_down)
        loop(4, edge)
        loop(16, cot_sum)
        loop(3, inputs)
        ig_v[...] = s["ig_acc"][...].astype(BF16).reshape(4, 4, 32, 256)

    stages = (stage0, stage1, stage2, stage3, stage4, stage5, stage6, stage7, stage8)
    flying = [[] for _ in range(CHUNKS)]
    for stage in stages:
        for k in range(CHUNKS):
            for copy in flying[k]:
                copy.wait_recv()
            before = flying[k]
            flying[k] = stage(k)
            for copy in before:
                copy.wait_send()
        if stage is stage1:
            input_grad()
            for copy, sends in halos:

                @pl.when(sends)
                def _(copy=copy):
                    copy.wait_send()

        if stage is stage2:
            early()
        if stage is stage3:
            loop(2, section)
        if stage is stage4:
            loop(2, lambda t: section(t + 2))

def store(so_v, ig_v, s_v, tg_v, so, ig, sg, tg, sems):
    pairs = [(s_v.at[pl.ds(n * 32, 32)], sg.at[pl.ds(n * 32, 32)]) for n in range(9)]
    pairs += [(so_v.at[n], so.at[n]) for n in range(4)]
    pairs += [(tg_v.at[pl.ds(n * 32, 32)], tg.at[pl.ds(n * 32, 32)]) for n in range(3)]
    pairs.append((ig_v, ig))
    copies = [pltpu.make_async_copy(src, dst, sems.at[n]) for n, (src, dst) in enumerate(pairs)]
    for copy in copies:
        copy.start()
    for copy in copies:
        copy.wait()


def on_device(low_frames, spatial_weight, temporal_weight, cotangent):
    hbm = pl.BlockSpec(memory_space=pltpu.HBM)
    vmem = pl.BlockSpec(memory_space=pltpu.VMEM)
    shapes = (
        jax.ShapeDtypeStruct((4, 8, 64, 256), BF16),
        jax.ShapeDtypeStruct((4, 4, 32, 256), BF16),
        jax.ShapeDtypeStruct((288, 8, 256), F32),
        jax.ShapeDtypeStruct((96, 8, 256), F32),
    )
    held = pl.pallas_call(
        kernel,
        out_shape=tuple(pltpu.VMEM(a.shape, a.dtype) for a in shapes),
        in_specs=[hbm] * 4,
        out_specs=(vmem,) * 4,
        scratch_shapes=list(SCRATCH.values()),
        compiler_params=pltpu.CompilerParams(
            collective_id=0, has_side_effects=True, vmem_limit_bytes=52 << 20
        ),
        name="section",
    )(low_frames[0], spatial_weight.reshape(9, 256, 256), temporal_weight, cotangent[0])
    outs = pl.pallas_call(
        store,
        out_shape=shapes,
        in_specs=[vmem] * 4,
        out_specs=(hbm,) * 4,
        scratch_shapes=[pltpu.SemaphoreType.DMA((17,))],
        compiler_params=pltpu.CompilerParams(vmem_limit_bytes=4 << 20),
        name="store",
    )(*(pltpu.with_memory_space_constraint(a, pltpu.VMEM) for a in held))
    section_out, input_grad, spatial_grad, temporal_grad = outs
    return (
        section_out[None],
        input_grad[None],
        spatial_grad.reshape(3, 3, 256, 256),
        temporal_grad.reshape(3, 256, 256),
    )


def solution(mesh):
    in_specs = (P("dp", "tm", "height", None, None), P(), P(), P("dp", "tm", "height", None, None))
    out_specs = (P("dp", "tm", "height", None, None), P("dp", "tm", "height", None, None), P(), P())
    return jax.shard_map(
        on_device, mesh=mesh, in_specs=in_specs, out_specs=out_specs, check_vma=False
    )
```
